32 devices in a mesh: seq: 8 (over z, x), head: 4 (over y, core).
Axes of the slice: x: 2, y: 2, z: 4, core: 2. Of those that a mesh axis runs over, the one named last changes fastest.
Arguments:
- queries: bfloat16 [2, 8, 14336], P(None, 'seq', 'head'), may hold values from -150 to 150
- new_keys: bfloat16 [2, 8, 14336], P(None, 'seq', 'head'), may hold values from -6 to 6
- new_values: bfloat16 [2, 8, 14336], P(None, 'seq', 'head'), may hold values from -6 to 6
- cache_keys: bfloat16 [8192, 14336], P('seq', 'head'), may hold values from -6 to 6
- cache_values: bfloat16 [8192, 14336], P('seq', 'head'), may hold values from -6 to 6
- slopes: float32 [112], P('head'), may hold values from 7.324219e-05 to 0.025
- seg_blocks: int32 [8], replicated, may hold values from 1 to 32, 48 in all
- request_row: int32 [8], replicated, may hold values from 0 to 7, each once
- out_weight: bfloat16 [14336, 14336], P('head', 'seq'), may hold values from -0.046875 to 0.046875
- residual: bfloat16 [2, 8, 14336], P(None, 'head', 'seq'), may hold values from -6 to 6
Outputs:
- mixed: bfloat16 [2, 8, 14336], P(None, 'head', 'seq')
The draws below stay inside these ranges and needn't reach their ends.
Inputs may be any that keep to these rules, and one draw needn't show every extreme that they name: `seg_blocks`: the requests are packed in order from block 0; 48 blocks are used and the rest of the cache is unused. `request_row`: each query row belongs to exactly one request.
All inputs are finite; a program needn't handle non-finite values.
Results may differ from the reference program's by a relative error of at most 0.006.
Values may be sent and summed in bfloat16 or wider, within the bound.
A program may use at most 64 MiB of HBM per device.

```python
import math
import jax
import jax.numpy as jnp
import numpy as np
from jax import lax

HEADS = 112
HDIM = 128
D = 14336
BLK = 128
NBLK = 64
NCACHE = 8192
REQ = 8
MOST = 32
LIVE = 48


def draw_cache_keys(key, part):
    noise = jnp.clip(jax.random.normal(jax.random.fold_in(key, 11), (NCACHE, HEADS * HDIM), jnp.float32), -6.0, 6.0)
    return noise.astype(jnp.bfloat16)


def draw_queries(key, part):
    noise = jnp.clip(jax.random.normal(jax.random.fold_in(key, 13), (2, REQ, HEADS * HDIM), jnp.float32), -6.0, 6.0)
    return noise.astype(jnp.bfloat16)


def steps_of(key, extent, split, least, largest):
    gain, own = 1.0, jax.random.fold_in(key, 6)
    for dim, parts in split:
        steps = jnp.exp(jax.random.uniform(jax.random.fold_in(own, dim), (parts,), jnp.float32, least / len(split), largest / len(split)))
        gain = gain * jnp.repeat(steps, extent[dim] // parts).reshape([-1 if axis == dim else 1 for axis in range(len(extent))])
    return gain


def split_up(count, total, reach, lean):
    loads = [(1 << 20) // math.isqrt(rank ** lean) + 1 for rank in range(2, count + 1)]
    spare, holding = total - reach - (count - 1), [1] * (count - 1)
    while spare > 0:
        free = [i for i in range(count - 1) if holding[i] < reach]
        mass, left = sum([loads[i] for i in free]), spare
        for i in free:
            more = min(reach - holding[i], max(1, left * loads[i] // mass), spare)
            holding[i] = holding[i] + more
            spare = spare - more
    return np.array([reach] + holding)


def ragged(own_key, count, total, bound, slope):
    if count == 2:
        one = jax.random.randint(own_key, (), max(1, total - bound), min(bound, total - 1) + 1)
        return jnp.stack([one, total - one])
    lengths = jnp.asarray(split_up(count, total, bound, slope), jnp.int32)
    twos = (count - 1) // 2
    giver, receiver = lengths[1:1 + 2 * twos:2], lengths[2:2 + 2 * twos:2]
    slack = jnp.minimum(giver - 1, bound - receiver)
    moved = jax.random.randint(jax.random.fold_in(own_key, 1), (twos,), 0, 1 << 20) % (slack + 1)
    lengths = lengths.at[1:1 + 2 * twos:2].set(giver - moved).at[2:2 + 2 * twos:2].set(receiver + moved)
    return lengths[jax.random.permutation(jax.random.fold_in(own_key, 2), count)]


def centred(stream_key, dims, scale, bound, cuts=(), kind=jnp.bfloat16):
    drawn = scale * jax.random.normal(stream_key, dims, jnp.float32)
    if cuts:
        drawn = drawn * steps_of(stream_key, dims, cuts, -0.22, 0.18)
    return jnp.clip(drawn, -bound, bound).astype(kind)


def setup_inputs(seed: int = 0) -> dict:
    streams_of = jax.random.split(jax.random.key(seed), 11)
    queries = draw_queries(jax.random.fold_in(streams_of[10], 71), 0)
    new_keys = centred(streams_of[1], (2, REQ, HEADS * HDIM), 1.0, 6.0, ((1, 8), (2, 4)))
    new_values = centred(streams_of[2], (2, REQ, HEADS * HDIM), 1.0, 6.0, ((1, 8), (2, 4)))
    cache_keys = draw_cache_keys(jax.random.fold_in(streams_of[10], 71), 0)
    cache_values = centred(streams_of[4], (NCACHE, HEADS * HDIM), 1.0, 6.0, ((0, 8), (1, 4)))
    slopes = jnp.clip(jnp.exp(math.log(0.025) - 5.8328595 * jax.random.uniform(streams_of[5], (HEADS,), jnp.float32) ** steps_of(streams_of[5], (HEADS,), ((0, 4),), -0.2, 0.2)), 7.324219041038305e-05, 0.025)
    seg_blocks = ragged(streams_of[6], REQ, LIVE, MOST, 2).astype(jnp.int32)
    request_row = jax.random.permutation(streams_of[7], REQ).astype(jnp.int32)
    out_weight = centred(streams_of[8], (HEADS * HDIM, D), (HEADS * HDIM) ** -0.5, 0.046875, ((0, 4), (1, 8)))
    residual = centred(streams_of[9], (2, REQ, D), 1.0, 6.0, ((1, 4), (2, 8)))
    return dict(queries=queries, new_keys=new_keys, new_values=new_values, cache_keys=cache_keys, cache_values=cache_values, slopes=slopes, seg_blocks=seg_blocks, request_row=request_row, out_weight=out_weight, residual=residual)


NEG = -1e+30

def self_terms(q, k, v, slopes, scale):
    q = q.astype(jnp.float32)
    k = k.astype(jnp.float32)
    v = v.astype(jnp.float32)
    first = lax.optimization_barrier(jnp.sum(q[0] * k[0], axis=-1)) * scale
    cross = lax.optimization_barrier(jnp.sum(q[1] * k[0], axis=-1)) * scale - slopes
    second = lax.optimization_barrier(jnp.sum(q[1] * k[1], axis=-1)) * scale
    upper = jnp.maximum(cross, second)
    e_cross = jnp.exp(cross - upper)
    e_second = jnp.exp(second - upper)
    top = jnp.stack([first, upper])
    total = jnp.stack([jnp.ones_like(first), e_cross + e_second])
    acc = jnp.stack([v[0], e_cross[..., None] * v[0] + e_second[..., None] * v[1]])
    return (top, total, acc)

def reference(queries, new_keys, new_values, cache_keys, cache_values, slopes, seg_blocks, request_row, out_weight, residual):
    scale = 1.0 / math.sqrt(HDIM)
    starts = jnp.cumsum(seg_blocks) - seg_blocks
    index = jnp.arange(NBLK, dtype=jnp.int32)
    hit = (index[:, None] >= starts[None, :]) & (index[:, None] < (starts + seg_blocks)[None, :])
    live = jnp.any(hit, axis=1)
    block_row = lax.optimization_barrier(jnp.sum(jnp.where(hit, request_row[None, :], 0), axis=1)).astype(jnp.int32)
    first = lax.optimization_barrier(jnp.sum(jnp.where(hit, starts[None, :], 0), axis=1)).astype(jnp.int32)
    length = lax.optimization_barrier(jnp.sum(jnp.where(hit, seg_blocks[None, :], 0), axis=1)).astype(jnp.int32)
    base = (length * BLK - (index - first) * BLK).astype(jnp.int32)
    block_query = jnp.take(queries, block_row, axis=1).reshape(2, NBLK, HEADS, HDIM).transpose(1, 0, 2, 3)
    keys = cache_keys.reshape(NBLK, BLK, HEADS, HDIM)
    values = cache_values.reshape(NBLK, BLK, HEADS, HDIM)

    def block_term(args):
        keys_b, values_b, query_b, base_b, live_b = args
        scores = jnp.einsum('shd,thd->sht', query_b.astype(jnp.float32), keys_b.astype(jnp.float32)) * scale
        dist = (base_b + jnp.arange(2, dtype=jnp.int32)[:, None] - jnp.arange(BLK, dtype=jnp.int32)[None, :]).astype(jnp.float32)
        scores = scores - slopes[None, :, None] * dist[:, None, :]
        top = lax.optimization_barrier(jnp.max(scores, axis=-1))
        probs = jnp.exp(scores - top[..., None])
        total = lax.optimization_barrier(jnp.sum(probs, axis=-1))
        weights = probs.astype(jnp.bfloat16)
        acc = jnp.einsum('sht,thd->shd', weights.astype(jnp.float32), values_b.astype(jnp.float32))
        top = jnp.where(live_b, top, NEG)
        total = jnp.where(live_b, total, 0.0)
        acc = jnp.where(live_b, acc, 0.0)
        return (top, total, acc)
    tops, totals, accs = lax.map(block_term, (keys, values, block_query, base, live))
    rowhot = (block_row[:, None] == jnp.arange(REQ, dtype=jnp.int32)[None, :]) & live[:, None]
    tab_top = lax.optimization_barrier(jnp.max(jnp.where(rowhot[:, :, None, None], tops[:, None], NEG), axis=0))
    ratio = jnp.exp(tops - jnp.take(tab_top, block_row, axis=0))
    tab_sum = jax.ops.segment_sum(ratio * totals, block_row, num_segments=REQ)
    tab_acc = jax.ops.segment_sum(ratio[..., None] * accs, block_row, num_segments=REQ)
    tab_top = tab_top.transpose(1, 0, 2)
    tab_sum = tab_sum.transpose(1, 0, 2)
    tab_acc = tab_acc.transpose(1, 0, 2, 3)
    own_top, own_sum, own_acc = self_terms(queries.reshape(2, REQ, HEADS, HDIM), new_keys.reshape(2, REQ, HEADS, HDIM), new_values.reshape(2, REQ, HEADS, HDIM), slopes, scale)
    top = jnp.maximum(tab_top, own_top)
    wa = jnp.exp(tab_top - top)
    wb = jnp.exp(own_top - top)
    total = tab_sum * wa + own_sum * wb
    acc = tab_acc * wa[..., None] + own_acc * wb[..., None]
    attended = (acc / total[..., None]).astype(jnp.bfloat16).reshape(2 * REQ, HEADS * HDIM)
    projected = jnp.dot(attended, out_weight, preferred_element_type=jnp.float32).reshape(2, REQ, D)
    return (residual.astype(jnp.float32) + projected).astype(jnp.bfloat16)
```

```python
import functools
import math

import jax
import jax.numpy as jnp
from jax import lax
from jax.experimental import pallas as pl
from jax.experimental.pallas import tpu as pltpu
from jax.sharding import PartitionSpec as P

BLK = 128
FAR = 1e35
LAG = 3
PARTS = 2
MESH = pl.DeviceIdType.MESH


def kernel(
    n_seq,
    n_head,
    heads,
    unit,
    tile,
    live,
    first,
    mergers,
    qry_ref,
    key_ref,
    val_ref,
    seg_ref,
    row_ref,
    slope_ref,
    res_ref,
    k_hbm,
    v_hbm,
    w_hbm,
    out_ref,
    kbuf,
    vbuf,
    wbuf,
    qall,
    kvown,
    own2d,
    qx,
    sbuf,
    pbuf,
    q2d,
    dist,
    o2d,
    st2d,
    sendb,
    recvb,
    xin,
    sofar,
    shares,
    got,
    k_sem,
    v_sem,
    w_sem,
    q_send,
    q_recv,
    kv_send,
    kv_recv,
    p_send,
    p_recv,
    a_send,
    a_recv,
    h_send,
    h_recv,
):
    hdim = qry_ref.shape[1] // heads
    rows = 2 * n_seq
    per = n_seq // n_head
    owned = n_seq // mergers
    tokens = k_hbm.shape[0]
    groups = heads // unit
    some = heads // PARTS
    slot = q2d.shape[0] // (2 * owned)
    wide = unit * hdim
    cols = w_hbm.shape[1]
    scale = 1.0 / math.sqrt(hdim)
    me = lax.axis_index("seq")
    mine = lax.axis_index("head")
    is_live = me < live
    is_merger = (me >= first) & (me < first + mergers)

    def k_copy(g):
        at = pl.ds(pl.multiple_of(g * wide, 128), wide)
        return pltpu.make_async_copy(k_hbm.at[:, at], kbuf.at[:, at], k_sem.at[g])

    def v_copy(g):
        at = pl.ds(pl.multiple_of(g * wide, 128), wide)
        return pltpu.make_async_copy(v_hbm.at[:, at], vbuf.at[:, at], v_sem.at[g])

    def w_copy(g):
        at = pl.ds(pl.multiple_of(g * wide, 128), wide)
        return pltpu.make_async_copy(w_hbm.at[at], wbuf.at[at], w_sem.at[g])

    def to_seq(step):
        return lax.rem(me + step, n_seq)

    def to_live(step):
        return lax.rem(me + step, live)

    def to_head(step):
        return lax.rem(mine + step, n_head)

    def remote(src, dst, send, recv, axis, to):
        return pltpu.make_async_remote_copy(
            src_ref=src,
            dst_ref=dst,
            send_sem=send,
            recv_sem=recv,
            device_id={axis: to},
            device_id_type=MESH,
        )

    barrier = pltpu.get_barrier_semaphore()

    @pl.when(is_live)
    def _():
        for step in range(1, n_seq):
            pl.semaphore_signal(
                barrier, inc=1, device_id={"seq": to_seq(step)}, device_id_type=MESH
            )

    for step in range(1, n_head):
        pl.semaphore_signal(
            barrier, inc=1, device_id={"head": to_head(step)}, device_id_type=MESH
        )

    @pl.when(is_live)
    def _():
        for g in range(groups):
            k_copy(g).start()
            v_copy(g).start()

    for g in range(groups):
        w_copy(g).start()

    def q_copy(n, to):
        return remote(qry_ref, qall.at[me], q_send.at[n], q_recv.at[me], "seq", to)

    @pl.when(is_live)
    def _():
        pl.semaphore_wait(barrier, live - 1 + n_head - 1)
        for step in range(1, live):
            q_copy(step - 1, to_live(step)).start()

    @pl.when(jnp.logical_not(is_live))
    def _():
        pl.semaphore_wait(barrier, live + n_head - 1)
        for d in range(live):
            q_copy(d, d).start()

    keeper = first + lax.div(me, owned)
    place = lax.rem(me, owned)

    def kv_copy(n, slot):
        ref = (key_ref, val_ref)[n]
        return remote(
            ref, kvown.at[slot, n], kv_send.at[n], kv_recv.at[slot, n], "seq", keeper
        )

    @pl.when(keeper != me)
    def _():
        for n in range(2):
            kv_copy(n, place).start()

    @pl.when(keeper == me)
    def _():
        kvown[place, 0] = key_ref[...]
        kvown[place, 1] = val_ref[...]

    lane = lax.broadcasted_iota(jnp.int32, (some, hdim), 1)
    hline = lax.broadcasted_iota(jnp.int32, (some, 1), 0)

    def lanes(h):
        return slice(h * hdim, (h + 1) * hdim)

    def lines(h):
        return slice(h * rows, (h + 1) * rows)

    def p_copy(p, m):
        return remote(
            sendb.at[m, p], recvb.at[me, p], p_send.at[p, m], p_recv.at[p, me], "seq", first + m
        )

    @pl.when(is_live)
    def attend():
        line = lax.broadcasted_iota(jnp.int32, (rows, 1), 0)
        begin = jnp.zeros((rows, 1), jnp.int32)
        end = jnp.zeros((rows, 1), jnp.int32)
        at = jnp.int32(0)
        for i in range(n_seq):
            after = at + seg_ref[i]
            hit = (line // 2) == row_ref[i]
            begin = jnp.where(hit, at * BLK, begin)
            end = jnp.where(hit, after * BLK, end)
            at = after
        token = me * tokens + lax.broadcasted_iota(jnp.int32, (rows, tokens), 1)
        gap = (end + lax.rem(line, 2) - token).astype(jnp.float32)
        dist[...] = jnp.where((token >= begin) & (token < end), gap, FAR)
        odd = lax.rem(lax.broadcasted_iota(jnp.int32, (rows, hdim), 1), 2) == 1

        for g in range(groups):
            k_copy(g).wait()
            v_copy(g).wait()
        qall[me] = qry_ref[...]
        for step in range(1, n_seq):
            source = to_seq(step)
            remote(
                qry_ref, qall.at[source], q_send.at[0], q_recv.at[source], "seq", source
            ).wait_recv()
        for r in range(n_seq):
            qx[2 * r : 2 * r + 2, :] = qall[r].astype(jnp.float32)

        def scores(h):
            dots = lax.dot_general(
                qx[:, lanes(h)].astype(jnp.bfloat16),
                kbuf[:, lanes(h)],
                (((1,), (1,)), ((), ())),
                preferred_element_type=jnp.float32,
            )
            sbuf[lines(h), :] = dots * scale - slope_ref[h] * dist[...]

        def soften(h):
            score = sbuf[lines(h), :]
            top = jnp.max(score, axis=-1, keepdims=True)
            prob = jnp.exp(score - top)
            total = jnp.sum(prob, axis=-1, keepdims=True)
            pbuf[lines(h), :] = prob.astype(jnp.bfloat16)
            st2d[lines(h), :] = jnp.where(odd, total, top)

        def weigh(h):
            o2d[lines(h), :] = jnp.dot(
                pbuf[lines(h), :], vbuf[:, lanes(h)], preferred_element_type=jnp.float32
            )

        def message(p):
            base = p * some * rows
            for m in range(mergers):
                stat = None
                for k in range(owned):
                    for s in range(2):
                        n = 2 * (m * owned + k) + s
                        x = st2d[pl.ds(base + n, some, stride=rows), :]
                        here = (lane // 16 == k) & (lax.rem(lane, 4) // 2 == s)
                        stat = x if stat is None else jnp.where(here, x, stat)
                        sendb[m, p, 2 * k + s] = o2d[
                            pl.ds(base + n, some, stride=rows), :
                        ].astype(jnp.bfloat16)
                high = stat.astype(jnp.bfloat16).astype(jnp.float32)
                rest = stat - high
                middle = rest.astype(jnp.bfloat16).astype(jnp.float32)
                low = rest - middle
                piece = lax.rem(lane, 16) // 4
                sendb[m, p, 2 * owned] = jnp.where(
                    piece == 0, high, jnp.where(piece == 1, middle, low)
                ).astype(jnp.bfloat16)

        for h in range(heads + 2 * LAG):
            if h < heads:
                scores(h)
            if 0 <= h - LAG < heads:
                soften(h - LAG)
            if 0 <= h - 2 * LAG:
                weigh(h - 2 * LAG)
            if h - 2 * LAG >= 0 and (h - 2 * LAG + 1) % some == 0:
                p = (h - 2 * LAG) // some
                message(p)
                for m in range(mergers):

                    @pl.when(me != first + m)
                    def _():
                        p_copy(p, m).start()

                    @pl.when(me == first + m)
                    def _():
                        recvb[me, p] = sendb[m, p]

    group = me - first

    def a_copy(p, to, n):
        return remote(
            xin.at[group, p], xin.at[group, p], a_send.at[p, n], a_recv.at[p, group], "seq", to
        )

    @pl.when(is_merger)
    def combine():
        base = group * owned
        for k in range(owned):

            @pl.when(base + k != me)
            def _():
                for n in range(2):
                    kv_copy(n, k).wait_recv()

        for k in range(owned):
            parts = (qall.at[base + k], kvown.at[k, 0], kvown.at[k, 1])
            for n, ref in enumerate(parts):
                for h in range(heads):
                    own2d[k, n, 2 * h : 2 * h + 2, :] = ref[:, lanes(h)].astype(jnp.float32)

        def own_terms(k, p):
            own = [
                [own2d.at[k, n][pl.ds(2 * p * some + t, some, stride=2), :] for t in range(2)]
                for n in range(3)
            ]
            slope_col = jnp.zeros((some, 1), jnp.float32)
            for h in range(some):
                slope_col = jnp.where(hline == h, slope_ref[p * some + h], slope_col)
            e00 = jnp.sum(own[0][0] * own[1][0], axis=-1, keepdims=True) * scale
            e10 = jnp.sum(own[0][1] * own[1][0], axis=-1, keepdims=True) * scale - slope_col
            e11 = jnp.sum(own[0][1] * own[1][1], axis=-1, keepdims=True) * scale
            upper = jnp.maximum(e10, e11)
            w10 = jnp.exp(e10 - upper)
            w11 = jnp.exp(e11 - upper)
            j = lax.rem(lane, 4)
            stat = jnp.where(
                j == 0, e00, jnp.where(j == 1, 1.0, jnp.where(j == 2, upper, w10 + w11))
            )
            return stat, [own[2][0], w10 * own[2][0] + w11 * own[2][1]]

        own = [[own_terms(k, p) for k in range(owned)] for p in range(PARTS)]

        def merge(p):
            stat = own[p][0][0]
            for k in range(1, owned):
                stat = jnp.where(lane // 16 == k, own[p][k][0], stat)
            stats = [stat]
            for j in range(live):
                x = recvb[j, p, 2 * owned].astype(jnp.float32)
                x = x + pltpu.roll(x, hdim - 4, 1) + pltpu.roll(x, hdim - 8, 1)
                stats.append(x)
            highest = functools.reduce(jnp.maximum, stats)
            factors = [jnp.exp(jnp.minimum(x - highest, 0.0)) for x in stats]
            total = sum(f * pltpu.roll(x, hdim - 1, 1) for f, x in zip(factors, stats))
            inverse = 1.0 / total
            for k in range(owned):
                for s in range(2):
                    c = slice(16 * k + 2 * s, 16 * k + 2 * s + 1)
                    acc = factors[0][:, c] * own[p][k][1][s]
                    for j in range(live):
                        acc += factors[j + 1][:, c] * recvb[j, p, 2 * k + s].astype(jnp.float32)
                    n = k // per * 2 * per + s * per + k % per
                    q2d[pl.ds(n * slot, some), :] = acc * inverse[:, c]
            for h in range(some):
                xin[group, p, :, lanes(h)] = q2d[
                    pl.ds(h, 2 * owned, stride=slot), :
                ].astype(jnp.bfloat16)

        for p in range(PARTS):
            for step in range(1, live):
                source = to_live(step)
                remote(
                    sendb.at[0, p], recvb.at[source, p], p_send.at[p, 0], p_recv.at[p, source],
                    "seq", source,
                ).wait_recv()
            merge(p)
            for n in range(1, n_seq):
                a_copy(p, to_seq(n_seq - n), n - 1).start()

    for g in range(groups):
        w_copy(g).wait()

    def h_copy(c, step):
        at = slice(c * tile, (c + 1) * tile)
        return remote(
            shares.at[to_head(step), :, at],
            got.at[step - 1, :, at],
            h_send.at[c, step - 1],
            h_recv.at[c, step - 1],
            "head",
            to_head(step),
        )

    for p in range(PARTS):
        for m in range(mergers):

            @pl.when(me != first + m)
            def _():
                here = xin.at[m, p]
                remote(
                    here, here, a_send.at[p, 0], a_recv.at[p, m], "seq", first + m
                ).wait_recv()

        x = jnp.concatenate([xin[m, p] for m in range(mergers)], axis=0)
        deep = slice(p * some * hdim, (p + 1) * some * hdim)
        for c in range(cols // tile):
            at = slice(c * tile, (c + 1) * tile)
            part = jnp.dot(x, wbuf[deep, at], preferred_element_type=jnp.float32)
            if p > 0:
                part += sofar[:, at]
            if p < PARTS - 1:
                sofar[:, at] = part
                continue
            for k in range(n_head):
                shares[k, :, at] = part[2 * per * k : 2 * per * (k + 1)].astype(jnp.bfloat16)
            for step in range(1, n_head):
                h_copy(c, step).start()

    summed = shares[mine].astype(jnp.float32)
    for step in range(1, n_head):
        for c in range(cols // tile):
            h_copy(c, step).wait_recv()
        summed += got[step - 1].astype(jnp.float32)
    for s in range(2):
        out_ref[s] = (
            res_ref[s].astype(jnp.float32) + summed[s * per : (s + 1) * per]
        ).astype(jnp.bfloat16)

    @pl.when(is_live)
    def _():
        for step in range(1, live):
            q_copy(step - 1, to_live(step)).wait_send()
        for m in range(mergers):

            @pl.when(me != first + m)
            def _():
                for p in range(PARTS):
                    p_copy(p, m).wait_send()

    @pl.when(jnp.logical_not(is_live))
    def _():
        for d in range(live):
            q_copy(d, d).wait_send()

    @pl.when(keeper != me)
    def _():
        for n in range(2):
            kv_copy(n, place).wait_send()

    @pl.when(is_merger)
    def _():
        for p in range(PARTS):
            for n in range(1, n_seq):
                a_copy(p, to_seq(n_seq - n), n - 1).wait_send()

    for step in range(1, n_head):
        for c in range(cols // tile):
            h_copy(c, step).wait_send()


def body(
    n_seq,
    n_head,
    queries,
    new_keys,
    new_values,
    cache_keys,
    cache_values,
    slopes,
    seg_blocks,
    request_row,
    out_weight,
    residual,
):
    heads = slopes.shape[0]
    width = queries.shape[2]
    hdim = width // heads
    tokens = cache_keys.shape[0]
    cols = out_weight.shape[1]
    assert queries.shape[1] == 1 and seg_blocks.shape[0] == n_seq
    flat = [x.reshape(2, width) for x in (queries, new_keys, new_values)]
    unit = max(u for u in (1, 2, 4) if heads % u == 0)
    tile = 256 if cols % 256 == 0 else cols
    rows = 2 * n_seq
    per = n_seq // n_head
    some = heads // PARTS
    slot = -(-some // 8) * 8
    live, first, mergers = 3 * n_seq // 4, n_seq // 4, n_seq // 4
    owned = n_seq // mergers
    assert n_seq % 4 == 0 and owned % per == 0 and 16 * owned <= hdim
    assert heads % PARTS == 0
    groups = heads // unit
    bf16, f32 = jnp.bfloat16, jnp.float32
    dma = pltpu.SemaphoreType.DMA
    vmem = pl.BlockSpec(memory_space=pltpu.VMEM)
    smem = pl.BlockSpec(memory_space=pltpu.SMEM)
    hbm = pl.BlockSpec(memory_space=pl.ANY)
    return pl.pallas_call(
        functools.partial(kernel, n_seq, n_head, heads, unit, tile, live, first, mergers),
        out_shape=jax.ShapeDtypeStruct(residual.shape, residual.dtype),
        in_specs=[vmem, vmem, vmem, smem, smem, smem, vmem, hbm, hbm, hbm],
        out_specs=vmem,
        scratch_shapes=[
            pltpu.VMEM(cache_keys.shape, bf16),
            pltpu.VMEM(cache_values.shape, bf16),
            pltpu.VMEM(out_weight.shape, bf16),
            pltpu.VMEM((n_seq, 2, width), bf16),
            pltpu.VMEM((owned, 2, 2, width), bf16),
            pltpu.VMEM((owned, 3, 2 * heads, hdim), f32),
            pltpu.VMEM((rows, width), f32),
            pltpu.VMEM((heads * rows, tokens), f32),
            pltpu.VMEM((heads * rows, tokens), bf16),
            pltpu.VMEM((2 * owned * slot, hdim), f32),
            pltpu.VMEM((rows, tokens), f32),
            pltpu.VMEM((heads * rows, hdim), f32),
            pltpu.VMEM((heads * rows, hdim), f32),
            pltpu.VMEM((mergers, PARTS, 2 * owned + 1, some, hdim), bf16),
            pltpu.VMEM((live, PARTS, 2 * owned + 1, some, hdim), bf16),
            pltpu.VMEM((mergers, PARTS, 2 * owned, some * hdim), bf16),
            pltpu.VMEM((rows, cols), f32),
            pltpu.VMEM((n_head, 2 * per, cols), bf16),
            pltpu.VMEM((n_head - 1, 2 * per, cols), bf16),
            dma((groups,)),
            dma((groups,)),
            dma((groups,)),
            dma((live,)),
            dma((n_seq,)),
            dma((2,)),
            dma((owned, 2)),
            dma((PARTS, mergers)),
            dma((PARTS, live)),
            dma((PARTS, n_seq - 1)),
            dma((PARTS, mergers)),
            dma((cols // tile, n_head - 1)),
            dma((cols // tile, n_head - 1)),
        ],
        compiler_params=pltpu.CompilerParams(
            collective_id=0, has_side_effects=True, vmem_limit_bytes=56 << 20
        ),
    )(*flat, seg_blocks, request_row, slopes, residual, cache_keys, cache_values, out_weight)


def solution(mesh):
    in_specs = (
        P(None, "seq", "head"),
        P(None, "seq", "head"),
        P(None, "seq", "head"),
        P("seq", "head"),
        P("seq", "head"),
        P("head"),
        P(),
        P(),
        P("head", "seq"),
        P(None, "head", "seq"),
    )
    out_specs = P(None, "head", "seq")
    sizes = (mesh.shape["seq"], mesh.shape["head"])
    return jax.shard_map(
        functools.partial(body, *sizes),
        mesh=mesh,
        in_specs=in_specs,
        out_specs=out_specs,
        check_vma=False,
    )
```

```python
import functools
import math

import jax
import jax.numpy as jnp
from jax import lax
from jax.experimental import pallas as pl
from jax.experimental.pallas import tpu as pltpu
from jax.sharding import PartitionSpec as P

BLK = 128
FAR = 1e35
LAG = 3
PARTS = 2
MESH = pl.DeviceIdType.MESH


def kernel(
    n_seq,
    n_head,
    heads,
    unit,
    tile,
    live,
    first,
    mergers,
    qry_ref,
    key_ref,
    val_ref,
    seg_ref,
    row_ref,
    slope_ref,
    res_ref,
    k_hbm,
    v_hbm,
    w_hbm,
    out_ref,
    kbuf,
    vbuf,
    wbuf,
    qall,
    kvown,
    own2d,
    qx,
    sbuf,
    pbuf,
    q2d,
    dist,
    o2d,
    st2d,
    sendb,
    recvb,
    xin,
    sofar,
    shares,
    got,
    k_sem,
    v_sem,
    w_sem,
    q_send,
    q_recv,
    kv_send,
    kv_recv,
    p_send,
    p_recv,
    a_send,
    a_recv,
    h_send,
    h_recv,
):
    hdim = qry_ref.shape[1] // heads
    rows = 2 * n_seq
    per = n_seq // n_head
    owned = n_seq // mergers
    tokens = k_hbm.shape[0]
    groups = heads // unit
    some = heads // PARTS
    slot = q2d.shape[0] // (2 * owned)
    wide = unit * hdim
    cols = w_hbm.shape[1]
    scale = 1.0 / math.sqrt(hdim)
    me = lax.axis_index("seq")
    mine = lax.axis_index("head")
    is_live = me < live
    is_merger = (me >= first) & (me < first + mergers)

    def k_copy(g):
        at = pl.ds(pl.multiple_of(g * wide, 128), wide)
        return pltpu.make_async_copy(k_hbm.at[:, at], kbuf.at[:, at], k_sem.at[g])

    def v_copy(g):
        at = pl.ds(pl.multiple_of(g * wide, 128), wide)
        return pltpu.make_async_copy(v_hbm.at[:, at], vbuf.at[:, at], v_sem.at[g])

    def w_copy(g):
        at = pl.ds(pl.multiple_of(g * wide, 128), wide)
        return pltpu.make_async_copy(w_hbm.at[at], wbuf.at[at], w_sem.at[g])

    def to_seq(step):
        return lax.rem(me + step, n_seq)

    def to_live(step):
        return lax.rem(me + step, live)

    def to_head(step):
        return lax.rem(mine + step, n_head)

    def remote(src, dst, send, recv, axis, to):
        return pltpu.make_async_remote_copy(
            src_ref=src,
            dst_ref=dst,
            send_sem=send,
            recv_sem=recv,
            device_id={axis: to},
            device_id_type=MESH,
        )

    @pl.when(is_live)
    def _():
        for g in range(groups):
            k_copy(g).start()
            v_copy(g).start()

    @pl.when(jnp.logical_not(is_live))
    def _():
        for g in range(groups):
            w_copy(g).start()

    barrier = pltpu.get_barrier_semaphore()

    @pl.when(is_live)
    def _():
        for step in range(1, n_seq):
            pl.semaphore_signal(
                barrier, inc=1, device_id={"seq": to_seq(step)}, device_id_type=MESH
            )

    for step in range(1, n_head):
        pl.semaphore_signal(
            barrier, inc=1, device_id={"head": to_head(step)}, device_id_type=MESH
        )

    def q_copy(n, to):
        return remote(qry_ref, qall.at[me], q_send.at[n], q_recv.at[me], "seq", to)

    @pl.when(is_live)
    def _():
        pl.semaphore_wait(barrier, live - 1 + n_head - 1)
        for step in range(1, live):
            q_copy(step - 1, to_live(step)).start()

    @pl.when(jnp.logical_not(is_live))
    def _():
        pl.semaphore_wait(barrier, live + n_head - 1)
        for d in range(live):
            q_copy(d, d).start()

    keeper = first + lax.div(me, owned)
    place = lax.rem(me, owned)

    def kv_copy(n, slot):
        ref = (key_ref, val_ref)[n]
        return remote(
            ref, kvown.at[slot, n], kv_send.at[n], kv_recv.at[slot, n], "seq", keeper
        )

    @pl.when(keeper != me)
    def _():
        for n in range(2):
            kv_copy(n, place).start()

    @pl.when(keeper == me)
    def _():
        kvown[place, 0] = key_ref[...]
        kvown[place, 1] = val_ref[...]

    lane = lax.broadcasted_iota(jnp.int32, (some, hdim), 1)
    hline = lax.broadcasted_iota(jnp.int32, (some, 1), 0)

    def lanes(h):
        return slice(h * hdim, (h + 1) * hdim)

    def lines(h):
        return slice(h * rows, (h + 1) * rows)

    def p_copy(p, m):
        return remote(
            sendb.at[m, p], recvb.at[me, p], p_send.at[p, m], p_recv.at[p, me], "seq", first + m
        )

    @pl.when(is_live)
    def attend():
        line = lax.broadcasted_iota(jnp.int32, (rows, 1), 0)
        begin = jnp.zeros((rows, 1), jnp.int32)
        end = jnp.zeros((rows, 1), jnp.int32)
        at = jnp.int32(0)
        for i in range(n_seq):
            after = at + seg_ref[i]
            hit = (line // 2) == row_ref[i]
            begin = jnp.where(hit, at * BLK, begin)
            end = jnp.where(hit, after * BLK, end)
            at = after
        token = me * tokens + lax.broadcasted_iota(jnp.int32, (rows, tokens), 1)
        gap = (end + lax.rem(line, 2) - token).astype(jnp.float32)
        dist[...] = jnp.where((token >= begin) & (token < end), gap, FAR)
        odd = lax.rem(lax.broadcasted_iota(jnp.int32, (rows, hdim), 1), 2) == 1

        qall[me] = qry_ref[...]
        for step in range(1, n_seq):
            source = to_seq(step)
            remote(
                qry_ref, qall.at[source], q_send.at[0], q_recv.at[source], "seq", source
            ).wait_recv()
        for r in range(n_seq):
            qx[2 * r : 2 * r + 2, :] = qall[r].astype(jnp.float32)

        def scores(h):
            dots = lax.dot_general(
                qx[:, lanes(h)].astype(jnp.bfloat16),
                kbuf[:, lanes(h)],
                (((1,), (1,)), ((), ())),
                preferred_element_type=jnp.float32,
            )
            sbuf[lines(h), :] = dots * scale - slope_ref[h] * dist[...]

        def soften(h):
            score = sbuf[lines(h), :]
            top = jnp.max(score, axis=-1, keepdims=True)
            prob = jnp.exp(score - top)
            total = jnp.sum(prob, axis=-1, keepdims=True)
            pbuf[lines(h), :] = prob.astype(jnp.bfloat16)
            st2d[lines(h), :] = jnp.where(odd, total, top)

        def weigh(h):
            o2d[lines(h), :] = jnp.dot(
                pbuf[lines(h), :], vbuf[:, lanes(h)], preferred_element_type=jnp.float32
            )

        def message(p):
            base = p * some * rows
            for m in range(mergers):
                stat = None
                for k in range(owned):
                    for s in range(2):
                        n = 2 * (m * owned + k) + s
                        x = st2d[pl.ds(base + n, some, stride=rows), :]
                        here = (lane // 16 == k) & (lax.rem(lane, 4) // 2 == s)
                        stat = x if stat is None else jnp.where(here, x, stat)
                        sendb[m, p, 2 * k + s] = o2d[
                            pl.ds(base + n, some, stride=rows), :
                        ].astype(jnp.bfloat16)
                high = stat.astype(jnp.bfloat16).astype(jnp.float32)
                rest = stat - high
                middle = rest.astype(jnp.bfloat16).astype(jnp.float32)
                low = rest - middle
                piece = lax.rem(lane, 16) // 4
                sendb[m, p, 2 * owned] = jnp.where(
                    piece == 0, high, jnp.where(piece == 1, middle, low)
                ).astype(jnp.bfloat16)

        for h in range(heads + 2 * LAG):
            if h % some == 0 and h < heads:
                for g in range(h // unit, (h + some) // unit):
                    k_copy(g).wait()
                    v_copy(g).wait()
                if h + some == heads:
                    for g in range(groups):
                        w_copy(g).start()
            if h < heads:
                scores(h)
            if 0 <= h - LAG < heads:
                soften(h - LAG)
            if 0 <= h - 2 * LAG:
                weigh(h - 2 * LAG)
            if h - 2 * LAG >= 0 and (h - 2 * LAG + 1) % some == 0:
                p = (h - 2 * LAG) // some
                message(p)
                for m in range(mergers):

                    @pl.when(me != first + m)
                    def _():
                        p_copy(p, m).start()

                    @pl.when(me == first + m)
                    def _():
                        recvb[me, p] = sendb[m, p]

    group = me - first

    def a_copy(p, to, n):
        return remote(
            xin.at[group, p], xin.at[group, p], a_send.at[p, n], a_recv.at[p, group], "seq", to
        )

    @pl.when(is_merger)
    def combine():
        base = group * owned
        for k in range(owned):

            @pl.when(base + k != me)
            def _():
                for n in range(2):
                    kv_copy(n, k).wait_recv()

        for k in range(owned):
            parts = (qall.at[base + k], kvown.at[k, 0], kvown.at[k, 1])
            for n, ref in enumerate(parts):
                for h in range(heads):
                    own2d[k, n, 2 * h : 2 * h + 2, :] = ref[:, lanes(h)].astype(jnp.float32)

        def own_terms(k, p):
            own = [
                [own2d.at[k, n][pl.ds(2 * p * some + t, some, stride=2), :] for t in range(2)]
                for n in range(3)
            ]
            slope_col = jnp.zeros((some, 1), jnp.float32)
            for h in range(some):
                slope_col = jnp.where(hline == h, slope_ref[p * some + h], slope_col)
            e00 = jnp.sum(own[0][0] * own[1][0], axis=-1, keepdims=True) * scale
            e10 = jnp.sum(own[0][1] * own[1][0], axis=-1, keepdims=True) * scale - slope_col
            e11 = jnp.sum(own[0][1] * own[1][1], axis=-1, keepdims=True) * scale
            upper = jnp.maximum(e10, e11)
            w10 = jnp.exp(e10 - upper)
            w11 = jnp.exp(e11 - upper)
            j = lax.rem(lane, 4)
            stat = jnp.where(
                j == 0, e00, jnp.where(j == 1, 1.0, jnp.where(j == 2, upper, w10 + w11))
            )
            return stat, [own[2][0], w10 * own[2][0] + w11 * own[2][1]]

        own = [[own_terms(k, p) for k in range(owned)] for p in range(PARTS)]

        def merge(p):
            stat = own[p][0][0]
            for k in range(1, owned):
                stat = jnp.where(lane // 16 == k, own[p][k][0], stat)
            stats = [stat]
            for j in range(live):
                x = recvb[j, p, 2 * owned].astype(jnp.float32)
                x = x + pltpu.roll(x, hdim - 4, 1) + pltpu.roll(x, hdim - 8, 1)
                stats.append(x)
            highest = functools.reduce(jnp.maximum, stats)
            factors = [jnp.exp(jnp.minimum(x - highest, 0.0)) for x in stats]
            total = sum(f * pltpu.roll(x, hdim - 1, 1) for f, x in zip(factors, stats))
            inverse = 1.0 / total
            for k in range(owned):
                for s in range(2):
                    c = slice(16 * k + 2 * s, 16 * k + 2 * s + 1)
                    acc = factors[0][:, c] * own[p][k][1][s]
                    for j in range(live):
                        acc += factors[j + 1][:, c] * recvb[j, p, 2 * k + s].astype(jnp.float32)
                    n = k // per * 2 * per + s * per + k % per
                    q2d[pl.ds(n * slot, some), :] = acc * inverse[:, c]
            for h in range(some):
                xin[group, p, :, lanes(h)] = q2d[
                    pl.ds(h, 2 * owned, stride=slot), :
                ].astype(jnp.bfloat16)

        for p in range(PARTS):
            for step in range(1, live):
                source = to_live(step)
                remote(
                    sendb.at[0, p], recvb.at[source, p], p_send.at[p, 0], p_recv.at[p, source],
                    "seq", source,
                ).wait_recv()
            merge(p)
            for n in range(1, n_seq):
                a_copy(p, to_seq(n_seq - n), n - 1).start()

    for g in range(groups):
        w_copy(g).wait()

    def h_copy(c, step):
        at = slice(c * tile, (c + 1) * tile)
        return remote(
            shares.at[to_head(step), :, at],
            got.at[step - 1, :, at],
            h_send.at[c, step - 1],
            h_recv.at[c, step - 1],
            "head",
            to_head(step),
        )

    for p in range(PARTS):
        for m in range(mergers):

            @pl.when(me != first + m)
            def _():
                here = xin.at[m, p]
                remote(
                    here, here, a_send.at[p, 0], a_recv.at[p, m], "seq", first + m
                ).wait_recv()

        x = jnp.concatenate([xin[m, p] for m in range(mergers)], axis=0)
        deep = slice(p * some * hdim, (p + 1) * some * hdim)
        for c in range(cols // tile):
            at = slice(c * tile, (c + 1) * tile)
            part = jnp.dot(x, wbuf[deep, at], preferred_element_type=jnp.float32)
            if p > 0:
                part += sofar[:, at]
            if p < PARTS - 1:
                sofar[:, at] = part
                continue
            for k in range(n_head):
                shares[k, :, at] = part[2 * per * k : 2 * per * (k + 1)].astype(jnp.bfloat16)
            for step in range(1, n_head):
                h_copy(c, step).start()

    summed = shares[mine].astype(jnp.float32)
    for step in range(1, n_head):
        for c in range(cols // tile):
            h_copy(c, step).wait_recv()
        summed += got[step - 1].astype(jnp.float32)
    for s in range(2):
        out_ref[s] = (
            res_ref[s].astype(jnp.float32) + summed[s * per : (s + 1) * per]
        ).astype(jnp.bfloat16)

    @pl.when(is_live)
    def _():
        for step in range(1, live):
            q_copy(step - 1, to_live(step)).wait_send()
        for m in range(mergers):

            @pl.when(me != first + m)
            def _():
                for p in range(PARTS):
                    p_copy(p, m).wait_send()

    @pl.when(jnp.logical_not(is_live))
    def _():
        for d in range(live):
            q_copy(d, d).wait_send()

    @pl.when(keeper != me)
    def _():
        for n in range(2):
            kv_copy(n, place).wait_send()

    @pl.when(is_merger)
    def _():
        for p in range(PARTS):
            for n in range(1, n_seq):
                a_copy(p, to_seq(n_seq - n), n - 1).wait_send()

    for step in range(1, n_head):
        for c in range(cols // tile):
            h_copy(c, step).wait_send()


def body(
    n_seq,
    n_head,
    queries,
    new_keys,
    new_values,
    cache_keys,
    cache_values,
    slopes,
    seg_blocks,
    request_row,
    out_weight,
    residual,
):
    heads = slopes.shape[0]
    width = queries.shape[2]
    hdim = width // heads
    tokens = cache_keys.shape[0]
    cols = out_weight.shape[1]
    assert queries.shape[1] == 1 and seg_blocks.shape[0] == n_seq
    flat = [x.reshape(2, width) for x in (queries, new_keys, new_values)]
    unit = heads // 2
    tile = cols
    rows = 2 * n_seq
    per = n_seq // n_head
    some = heads // PARTS
    slot = -(-some // 8) * 8
    live, first, mergers = 3 * n_seq // 4, n_seq // 4, n_seq // 4
    owned = n_seq // mergers
    assert n_seq % 4 == 0 and owned % per == 0 and 16 * owned <= hdim
    assert heads % PARTS == 0
    groups = heads // unit
    bf16, f32 = jnp.bfloat16, jnp.float32
    dma = pltpu.SemaphoreType.DMA
    vmem = pl.BlockSpec(memory_space=pltpu.VMEM)
    smem = pl.BlockSpec(memory_space=pltpu.SMEM)
    hbm = pl.BlockSpec(memory_space=pl.ANY)
    return pl.pallas_call(
        functools.partial(kernel, n_seq, n_head, heads, unit, tile, live, first, mergers),
        out_shape=jax.ShapeDtypeStruct(residual.shape, residual.dtype),
        in_specs=[vmem, vmem, vmem, smem, smem, smem, vmem, hbm, hbm, hbm],
        out_specs=vmem,
        scratch_shapes=[
            pltpu.VMEM(cache_keys.shape, bf16),
            pltpu.VMEM(cache_values.shape, bf16),
            pltpu.VMEM(out_weight.shape, bf16),
            pltpu.VMEM((n_seq, 2, width), bf16),
            pltpu.VMEM((owned, 2, 2, width), bf16),
            pltpu.VMEM((owned, 3, 2 * heads, hdim), f32),
            pltpu.VMEM((rows, width), f32),
            pltpu.VMEM((heads * rows, tokens), f32),
            pltpu.VMEM((heads * rows, tokens), bf16),
            pltpu.VMEM((2 * owned * slot, hdim), f32),
            pltpu.VMEM((rows, tokens), f32),
            pltpu.VMEM((heads * rows, hdim), f32),
            pltpu.VMEM((heads * rows, hdim), f32),
            pltpu.VMEM((mergers, PARTS, 2 * owned + 1, some, hdim), bf16),
            pltpu.VMEM((live, PARTS, 2 * owned + 1, some, hdim), bf16),
            pltpu.VMEM((mergers, PARTS, 2 * owned, some * hdim), bf16),
            pltpu.VMEM((rows, cols), f32),
            pltpu.VMEM((n_head, 2 * per, cols), bf16),
            pltpu.VMEM((n_head - 1, 2 * per, cols), bf16),
            dma((groups,)),
            dma((groups,)),
            dma((groups,)),
            dma((live,)),
            dma((n_seq,)),
            dma((2,)),
            dma((owned, 2)),
            dma((PARTS, mergers)),
            dma((PARTS, live)),
            dma((PARTS, n_seq - 1)),
            dma((PARTS, mergers)),
            dma((cols // tile, n_head - 1)),
            dma((cols // tile, n_head - 1)),
        ],
        compiler_params=pltpu.CompilerParams(
            collective_id=0, has_side_effects=True, vmem_limit_bytes=56 << 20
        ),
    )(*flat, seg_blocks, request_row, slopes, residual, cache_keys, cache_values, out_weight)


def solution(mesh):
    in_specs = (
        P(None, "seq", "head"),
        P(None, "seq", "head"),
        P(None, "seq", "head"),
        P("seq", "head"),
        P("seq", "head"),
        P("head"),
        P(),
        P(),
        P("head", "seq"),
        P(None, "head", "seq"),
    )
    out_specs = P(None, "head", "seq")
    sizes = (mesh.shape["seq"], mesh.shape["head"])
    return jax.shard_map(
        functools.partial(body, *sizes),
        mesh=mesh,
        in_specs=in_specs,
        out_specs=out_specs,
        check_vma=False,
    )
```

```python
import functools
import math

import jax
import jax.numpy as jnp
from jax import lax
from jax.experimental import pallas as pl
from jax.experimental.pallas import tpu as pltpu
from jax.sharding import PartitionSpec as P

BLK = 128
FAR = 1e35
LAG = 3
MESH = pl.DeviceIdType.MESH


def kernel(
    n_seq,
    n_head,
    heads,
    unit,
    tile,
    live,
    first,
    mergers,
    sizes,
    qry_hbm,
    key_hbm,
    val_hbm,
    seg_hbm,
    row_hbm,
    slope_hbm,
    res_hbm,
    k_hbm,
    v_hbm,
    w_hbm,
    out_ref,
    qry_ref,
    key_ref,
    val_ref,
    seg_ref,
    row_ref,
    slope_ref,
    res_ref,
    i_sem,
    kbuf,
    vbuf,
    wbuf,
    qall,
    kvown,
    own2d,
    qx,
    sbuf,
    pbuf,
    q2d,
    dist,
    o2d,
    st2d,
    sendb,
    recvb,
    xin,
    sofar,
    shares,
    got,
    k_sem,
    v_sem,
    w_sem,
    q_send,
    q_recv,
    kv_send,
    kv_recv,
    p_send,
    p_recv,
    a_send,
    a_recv,
    h_send,
    h_recv,
):
    hdim = qry_ref.shape[1] // heads
    rows = 2 * n_seq
    per = n_seq // n_head
    owned = n_seq // mergers
    tokens = k_hbm.shape[0]
    groups = heads // unit
    parts = len(sizes)
    starts = [sum(sizes[:p]) for p in range(parts)]
    slot = q2d.shape[0] // (2 * owned)
    wide = unit * hdim
    cols = w_hbm.shape[1]
    scale = 1.0 / math.sqrt(hdim)
    me = lax.axis_index("seq")
    mine = lax.axis_index("head")
    is_live = me < live
    is_merger = (me >= first) & (me < first + mergers)

    def k_copy(g):
        at = pl.ds(pl.multiple_of(g * wide, 128), wide)
        return pltpu.make_async_copy(k_hbm.at[:, at], kbuf.at[:, at], k_sem.at[g])

    def v_copy(g):
        at = pl.ds(pl.multiple_of(g * wide, 128), wide)
        return pltpu.make_async_copy(v_hbm.at[:, at], vbuf.at[:, at], v_sem.at[g])

    def w_copy(g):
        at = pl.ds(pl.multiple_of(g * wide, 128), wide)
        return pltpu.make_async_copy(w_hbm.at[at], wbuf.at[at], w_sem.at[g])

    staged = [
        pltpu.make_async_copy(src, dst, i_sem.at[n])
        for n, (src, dst) in enumerate(
            (
                (qry_hbm, qry_ref),
                (key_hbm, key_ref),
                (val_hbm, val_ref),
                (seg_hbm, seg_ref),
                (row_hbm, row_ref),
                (slope_hbm, slope_ref),
                (res_hbm, res_ref),
            )
        )
    ]

    def to_seq(step):
        return lax.rem(me + step, n_seq)

    def to_live(step):
        return lax.rem(me + step, live)

    def other(n):
        return n + jnp.where(me <= n, 1, 0)

    def to_head(step):
        return lax.rem(mine + step, n_head)

    def remote(src, dst, send, recv, axis, to):
        return pltpu.make_async_remote_copy(
            src_ref=src,
            dst_ref=dst,
            send_sem=send,
            recv_sem=recv,
            device_id={axis: to},
            device_id_type=MESH,
        )

    @pl.when(is_live)
    def _():
        for g in range(groups):
            k_copy(g).start()
            v_copy(g).start()

    barrier = pltpu.get_barrier_semaphore()

    @pl.when(is_live)
    def _():
        for step in range(1, n_seq):
            pl.semaphore_signal(
                barrier, inc=1, device_id={"seq": to_seq(step)}, device_id_type=MESH
            )

    for step in range(1, n_head):
        pl.semaphore_signal(
            barrier, inc=1, device_id={"head": to_head(step)}, device_id_type=MESH
        )

    for copy in staged:
        copy.start()

    def q_copy(n, to):
        return remote(qry_hbm, qall.at[me], q_send.at[n], q_recv.at[me], "seq", to)

    @pl.when(is_live)
    def _():
        pl.semaphore_wait(barrier, live - 1 + n_head - 1)
        for step in range(1, live):
            q_copy(step - 1, to_live(step)).start()

    @pl.when(jnp.logical_not(is_live))
    def _():
        pl.semaphore_wait(barrier, live + n_head - 1)
        for d in range(live):
            q_copy(d, d).start()
        for g in range(groups):
            w_copy(g).start()

    keeper = first + lax.div(me, owned)
    place = lax.rem(me, owned)

    def kv_copy(n, slot):
        ref = (key_hbm, val_hbm)[n]
        return remote(
            ref, kvown.at[slot, n], kv_send.at[n], kv_recv.at[slot, n], "seq", keeper
        )

    @pl.when(keeper != me)
    def _():
        for n in range(2):
            kv_copy(n, place).start()

    for copy in staged:
        copy.wait()

    @pl.when(keeper == me)
    def _():
        kvown[place, 0] = key_ref[...]
        kvown[place, 1] = val_ref[...]

    def lane_of(p):
        return lax.broadcasted_iota(jnp.int32, (sizes[p], hdim), 1)

    def lanes(h):
        return slice(h * hdim, (h + 1) * hdim)

    def lines(h):
        return slice(h * rows, (h + 1) * rows)

    def p_copy(p, m):
        return remote(
            sendb[p].at[m], recvb[p].at[me], p_send.at[p, m], p_recv.at[p, me], "seq", first + m
        )

    @pl.when(is_live)
    def attend():
        line = lax.broadcasted_iota(jnp.int32, (rows, 1), 0)
        begin = jnp.zeros((rows, 1), jnp.int32)
        end = jnp.zeros((rows, 1), jnp.int32)
        at = jnp.int32(0)
        for i in range(n_seq):
            after = at + seg_ref[i]
            hit = (line // 2) == row_ref[i]
            begin = jnp.where(hit, at * BLK, begin)
            end = jnp.where(hit, after * BLK, end)
            at = after
        token = me * tokens + lax.broadcasted_iota(jnp.int32, (rows, tokens), 1)
        gap = (end + lax.rem(line, 2) - token).astype(jnp.float32)
        dist[...] = jnp.where((token >= begin) & (token < end), gap, FAR)
        odd = lax.rem(lax.broadcasted_iota(jnp.int32, (rows, hdim), 1), 2) == 1

        qall[me] = qry_ref[...]
        for step in range(1, n_seq):
            source = to_seq(step)
            remote(
                qry_ref, qall.at[source], q_send.at[0], q_recv.at[source], "seq", source
            ).wait_recv()
        for r in range(n_seq):
            qx[2 * r : 2 * r + 2, :] = qall[r].astype(jnp.float32)

        def scores(h):
            dots = lax.dot_general(
                qx[:, lanes(h)].astype(jnp.bfloat16),
                kbuf[:, lanes(h)],
                (((1,), (1,)), ((), ())),
                preferred_element_type=jnp.float32,
            )
            sbuf[lines(h), :] = dots * scale - slope_ref[h] * dist[...]

        def soften(h):
            score = sbuf[lines(h), :]
            top = jnp.max(score, axis=-1, keepdims=True)
            prob = jnp.exp(score - top)
            total = jnp.sum(prob, axis=-1, keepdims=True)
            pbuf[lines(h), :] = prob.astype(jnp.bfloat16)
            st2d[lines(h), :] = jnp.where(odd, total, top)

        def weigh(h):
            o2d[lines(h), :] = jnp.dot(
                pbuf[lines(h), :], vbuf[:, lanes(h)], preferred_element_type=jnp.float32
            )

        def message(p):
            base, some, lane = starts[p] * rows, sizes[p], lane_of(p)
            for m in range(mergers):
                stat = None
                for k in range(owned):
                    for s in range(2):
                        n = 2 * (m * owned + k) + s
                        x = st2d[pl.ds(base + n, some, stride=rows), :]
                        here = (lane // 16 == k) & (lax.rem(lane, 4) // 2 == s)
                        stat = x if stat is None else jnp.where(here, x, stat)
                        sendb[p][m, 2 * k + s] = o2d[
                            pl.ds(base + n, some, stride=rows), :
                        ].astype(jnp.bfloat16)
                high = stat.astype(jnp.bfloat16).astype(jnp.float32)
                rest = stat - high
                middle = rest.astype(jnp.bfloat16).astype(jnp.float32)
                low = rest - middle
                piece = lax.rem(lane, 16) // 4
                sendb[p][m, 2 * owned] = jnp.where(
                    piece == 0, high, jnp.where(piece == 1, middle, low)
                ).astype(jnp.bfloat16)

        half = heads // 2 if groups % 2 == 0 else heads
        for h in range(heads + 2 * LAG):
            if h < heads and h % half == 0:
                for g in range(h // unit, (h + half) // unit):
                    k_copy(g).wait()
                    v_copy(g).wait()
                if h + half == heads:
                    for g in range(groups):
                        w_copy(g).start()
            if h < heads:
                scores(h)
            if 0 <= h - LAG < heads:
                soften(h - LAG)
            if 0 <= h - 2 * LAG:
                weigh(h - 2 * LAG)
            if h - 2 * LAG + 1 in starts[1:] + [heads]:
                p = (starts[1:] + [heads]).index(h - 2 * LAG + 1)
                message(p)
                for m in range(mergers):

                    @pl.when(me != first + m)
                    def _():
                        p_copy(p, m).start()

                    @pl.when(me == first + m)
                    def _():
                        recvb[p][me] = sendb[p][m]

    group = me - first

    def a_copy(p, to, n):
        return remote(
            xin[p].at[group], xin[p].at[group], a_send.at[p, n], a_recv.at[p, group], "seq", to
        )

    @pl.when(is_merger)
    def combine():
        base = group * owned
        for k in range(owned):

            @pl.when(base + k != me)
            def _():
                for n in range(2):
                    kv_copy(n, k).wait_recv()

        for k in range(owned):
            for n, ref in enumerate((qall.at[base + k], kvown.at[k, 0], kvown.at[k, 1])):
                for h in range(heads):
                    own2d[k, n, 2 * h : 2 * h + 2, :] = ref[:, lanes(h)].astype(jnp.float32)

        def own_terms(k, p):
            some, begin, lane = sizes[p], starts[p], lane_of(p)
            hline = lax.broadcasted_iota(jnp.int32, (some, 1), 0)
            own = [
                [own2d.at[k, n][pl.ds(2 * begin + t, some, stride=2), :] for t in range(2)]
                for n in range(3)
            ]
            slope_col = jnp.zeros((some, 1), jnp.float32)
            for h in range(some):
                slope_col = jnp.where(hline == h, slope_ref[begin + h], slope_col)
            e00 = jnp.sum(own[0][0] * own[1][0], axis=-1, keepdims=True) * scale
            e10 = jnp.sum(own[0][1] * own[1][0], axis=-1, keepdims=True) * scale - slope_col
            e11 = jnp.sum(own[0][1] * own[1][1], axis=-1, keepdims=True) * scale
            upper = jnp.maximum(e10, e11)
            w10 = jnp.exp(e10 - upper)
            w11 = jnp.exp(e11 - upper)
            j = lax.rem(lane, 4)
            stat = jnp.where(
                j == 0, e00, jnp.where(j == 1, 1.0, jnp.where(j == 2, upper, w10 + w11))
            )
            return stat, [own[2][0], w10 * own[2][0] + w11 * own[2][1]]

        own = [[own_terms(k, p) for k in range(owned)] for p in range(parts)]

        def merge(p):
            some, lane = sizes[p], lane_of(p)
            stat = own[p][0][0]
            for k in range(1, owned):
                stat = jnp.where(lane // 16 == k, own[p][k][0], stat)
            stats = [stat]
            for j in range(live):
                x = recvb[p][j, 2 * owned].astype(jnp.float32)
                x = x + pltpu.roll(x, hdim - 4, 1) + pltpu.roll(x, hdim - 8, 1)
                stats.append(x)
            highest = functools.reduce(jnp.maximum, stats)
            factors = [jnp.exp(jnp.minimum(x - highest, 0.0)) for x in stats]
            total = sum(f * pltpu.roll(x, hdim - 1, 1) for f, x in zip(factors, stats))
            inverse = 1.0 / total
            for k in range(owned):
                for s in range(2):
                    c = slice(16 * k + 2 * s, 16 * k + 2 * s + 1)
                    acc = factors[0][:, c] * own[p][k][1][s]
                    for j in range(live):
                        acc += factors[j + 1][:, c] * recvb[p][j, 2 * k + s].astype(jnp.float32)
                    n = k // per * 2 * per + s * per + k % per
                    q2d[pl.ds(n * slot, some), :] = acc * inverse[:, c]
            for h in range(some):
                xin[p][group, :, lanes(h)] = q2d[
                    pl.ds(h, 2 * owned, stride=slot), :
                ].astype(jnp.bfloat16)

        for p in range(parts):
            for step in range(1, live):
                source = to_live(step)
                remote(
                    sendb[p].at[0], recvb[p].at[source], p_send.at[p, 0], p_recv.at[p, source],
                    "seq", source,
                ).wait_recv()
            merge(p)
            for n in range(1, n_seq):
                a_copy(p, other(n - 1), n - 1).start()

    for g in range(groups):
        w_copy(g).wait()

    def h_copy(c, step):
        at = slice(c * tile, (c + 1) * tile)
        return remote(
            shares.at[to_head(step), :, at],
            got.at[step - 1, :, at],
            h_send.at[c, step - 1],
            h_recv.at[c, step - 1],
            "head",
            to_head(step),
        )

    for p in range(parts):
        for m in range(mergers):

            @pl.when(me != first + m)
            def _():
                here = xin[p].at[m]
                remote(
                    here, here, a_send.at[p, 0], a_recv.at[p, m], "seq", first + m
                ).wait_recv()

        x = jnp.concatenate([xin[p][m] for m in range(mergers)], axis=0)
        deep = slice(starts[p] * hdim, (starts[p] + sizes[p]) * hdim)
        for c in range(cols // tile):
            at = slice(c * tile, (c + 1) * tile)
            part = jnp.dot(x, wbuf[deep, at], preferred_element_type=jnp.float32)
            if p > 0:
                part += sofar[:, at]
            if p < parts - 1:
                sofar[:, at] = part
                continue
            for k in range(n_head):
                shares[k, :, at] = part[2 * per * k : 2 * per * (k + 1)].astype(jnp.bfloat16)
            for step in range(1, n_head):
                h_copy(c, step).start()

    summed = shares[mine].astype(jnp.float32)
    for step in range(1, n_head):
        for c in range(cols // tile):
            h_copy(c, step).wait_recv()
        summed += got[step - 1].astype(jnp.float32)
    for s in range(2):
        out_ref[s] = (
            res_ref[s].astype(jnp.float32) + summed[s * per : (s + 1) * per]
        ).astype(jnp.bfloat16)

    @pl.when(is_live)
    def _():
        for step in range(1, live):
            q_copy(step - 1, to_live(step)).wait_send()
        for m in range(mergers):

            @pl.when(me != first + m)
            def _():
                for p in range(parts):
                    p_copy(p, m).wait_send()

    @pl.when(jnp.logical_not(is_live))
    def _():
        for d in range(live):
            q_copy(d, d).wait_send()

    @pl.when(keeper != me)
    def _():
        for n in range(2):
            kv_copy(n, place).wait_send()

    @pl.when(is_merger)
    def _():
        for p in range(parts):
            for n in range(1, n_seq):
                a_copy(p, other(n - 1), n - 1).wait_send()

    for step in range(1, n_head):
        for c in range(cols // tile):
            h_copy(c, step).wait_send()


def body(
    n_seq,
    n_head,
    queries,
    new_keys,
    new_values,
    cache_keys,
    cache_values,
    slopes,
    seg_blocks,
    request_row,
    out_weight,
    residual,
):
    heads = slopes.shape[0]
    width = queries.shape[2]
    hdim = width // heads
    tokens = cache_keys.shape[0]
    cols = out_weight.shape[1]
    assert queries.shape[1] == 1 and seg_blocks.shape[0] == n_seq
    flat = [x.reshape(2, width) for x in (queries, new_keys, new_values)]
    unit = heads // 2
    tile = cols
    rows = 2 * n_seq
    per = n_seq // n_head
    sizes = (heads * 3 // 7, heads * 2 // 7, heads * 2 // 7)
    parts = len(sizes)
    slot = -(-max(sizes) // 8) * 8
    live, first, mergers = 3 * n_seq // 4, 0, n_head
    owned = n_seq // mergers
    assert n_seq % 4 == 0 and owned % per == 0 and 16 * owned <= hdim
    assert sum(sizes) == heads
    groups = heads // unit
    bf16, f32 = jnp.bfloat16, jnp.float32
    dma = pltpu.SemaphoreType.DMA
    vmem = pl.BlockSpec(memory_space=pltpu.VMEM)
    hbm = pl.BlockSpec(memory_space=pl.ANY)
    return pl.pallas_call(
        functools.partial(kernel, n_seq, n_head, heads, unit, tile, live, first, mergers, sizes),
        out_shape=jax.ShapeDtypeStruct(residual.shape, residual.dtype),
        in_specs=[hbm] * 10,
        out_specs=vmem,
        scratch_shapes=[
            pltpu.VMEM((2, width), bf16),
            pltpu.VMEM((2, width), bf16),
            pltpu.VMEM((2, width), bf16),
            pltpu.SMEM(seg_blocks.shape, jnp.int32),
            pltpu.SMEM(request_row.shape, jnp.int32),
            pltpu.SMEM(slopes.shape, f32),
            pltpu.VMEM(residual.shape, bf16),
            dma((7,)),
            pltpu.VMEM(cache_keys.shape, bf16),
            pltpu.VMEM(cache_values.shape, bf16),
            pltpu.VMEM(out_weight.shape, bf16),
            pltpu.VMEM((n_seq, 2, width), bf16),
            pltpu.VMEM((owned, 2, 2, width), bf16),
            pltpu.VMEM((owned, 3, 2 * heads, hdim), f32),
            pltpu.VMEM((rows, width), f32),
            pltpu.VMEM((heads * rows, tokens), f32),
            pltpu.VMEM((heads * rows, tokens), bf16),
            pltpu.VMEM((2 * owned * slot, hdim), f32),
            pltpu.VMEM((rows, tokens), f32),
            pltpu.VMEM((heads * rows, hdim), f32),
            pltpu.VMEM((heads * rows, hdim), f32),
            tuple(pltpu.VMEM((mergers, 2 * owned + 1, n, hdim), bf16) for n in sizes),
            tuple(pltpu.VMEM((live, 2 * owned + 1, n, hdim), bf16) for n in sizes),
            tuple(pltpu.VMEM((mergers, 2 * owned, n * hdim), bf16) for n in sizes),
            pltpu.VMEM((rows, cols), f32),
            pltpu.VMEM((n_head, 2 * per, cols), bf16),
            pltpu.VMEM((n_head - 1, 2 * per, cols), bf16),
            dma((groups,)),
            dma((groups,)),
            dma((groups,)),
            dma((live,)),
            dma((n_seq,)),
            dma((2,)),
            dma((owned, 2)),
            dma((parts, mergers)),
            dma((parts, live)),
            dma((parts, n_seq - 1)),
            dma((parts, mergers)),
            dma((cols // tile, n_head - 1)),
            dma((cols // tile, n_head - 1)),
        ],
        compiler_params=pltpu.CompilerParams(
            collective_id=0, has_side_effects=True, vmem_limit_bytes=56 << 20
        ),
    )(*flat, seg_blocks, request_row, slopes, residual, cache_keys, cache_values, out_weight)


def solution(mesh):
    in_specs = (
        P(None, "seq", "head"),
        P(None, "seq", "head"),
        P(None, "seq", "head"),
        P("seq", "head"),
        P("seq", "head"),
        P("head"),
        P(),
        P(),
        P("head", "seq"),
        P(None, "head", "seq"),
    )
    out_specs = P(None, "head", "seq")
    sizes = (mesh.shape["seq"], mesh.shape["head"])
    return jax.shard_map(
        functools.partial(body, *sizes),
        mesh=mesh,
        in_specs=in_specs,
        out_specs=out_specs,
        check_vma=False,
    )
```

```python
import functools
import math

import jax
import jax.numpy as jnp
from jax import lax
from jax.experimental import pallas as pl
from jax.experimental.pallas import tpu as pltpu
from jax.sharding import PartitionSpec as P

BLK = 128
FAR = 1e35
LAG = 3
MESH = pl.DeviceIdType.MESH


def kernel(
    n_seq,
    n_head,
    heads,
    unit,
    tile,
    live,
    first,
    mergers,
    sizes,
    qry_hbm,
    key_hbm,
    val_hbm,
    seg_hbm,
    row_hbm,
    slope_hbm,
    res_hbm,
    k_hbm,
    v_hbm,
    w_hbm,
    out_ref,
    qry_ref,
    key_ref,
    val_ref,
    seg_ref,
    row_ref,
    slope_ref,
    res_ref,
    i_sem,
    kbuf,
    kturn,
    vbuf,
    wbuf,
    qall,
    kvown,
    own2d,
    qx,
    sbuf,
    pbuf,
    q2d,
    dist,
    o2d,
    st2d,
    sendb,
    recvb,
    xin,
    sofar,
    shares,
    got,
    k_sem,
    v_sem,
    w_sem,
    q_send,
    q_recv,
    kv_send,
    kv_recv,
    p_send,
    p_recv,
    a_send,
    a_recv,
    h_send,
    h_recv,
):
    hdim = qry_ref.shape[1] // heads
    rows = 2 * n_seq
    per = n_seq // n_head
    owned = n_seq // mergers
    tokens = k_hbm.shape[0]
    groups = heads // unit
    parts = len(sizes)
    starts = [sum(sizes[:p]) for p in range(parts)]
    slot = q2d.shape[0] // (2 * owned)
    wide = unit * hdim
    cols = w_hbm.shape[1]
    scale = 1.0 / math.sqrt(hdim)
    me = lax.axis_index("seq")
    mine = lax.axis_index("head")
    is_live = me < live
    is_merger = (me >= first) & (me < first + mergers)

    def k_copy(g):
        at = pl.ds(pl.multiple_of(g * wide, 128), wide)
        return pltpu.make_async_copy(k_hbm.at[:, at], kbuf.at[:, at], k_sem.at[g])

    def v_copy(g):
        at = pl.ds(pl.multiple_of(g * wide, 128), wide)
        return pltpu.make_async_copy(v_hbm.at[:, at], vbuf.at[:, at], v_sem.at[g])

    def w_copy(g):
        at = pl.ds(pl.multiple_of(g * wide, 128), wide)
        return pltpu.make_async_copy(w_hbm.at[at], wbuf.at[at], w_sem.at[g])

    staged = [
        pltpu.make_async_copy(src, dst, i_sem.at[n])
        for n, (src, dst) in enumerate(
            (
                (qry_hbm, qry_ref),
                (key_hbm, key_ref),
                (val_hbm, val_ref),
                (seg_hbm, seg_ref),
                (row_hbm, row_ref),
                (slope_hbm, slope_ref),
                (res_hbm, res_ref),
            )
        )
    ]

    def to_seq(step):
        return lax.rem(me + step, n_seq)

    def to_live(step):
        return lax.rem(me + step, live)

    def other(n):
        return n + jnp.where(me <= n, 1, 0)

    def to_head(step):
        return lax.rem(mine + step, n_head)

    def remote(src, dst, send, recv, axis, to):
        return pltpu.make_async_remote_copy(
            src_ref=src,
            dst_ref=dst,
            send_sem=send,
            recv_sem=recv,
            device_id={axis: to},
            device_id_type=MESH,
        )

    @pl.when(is_live)
    def _():
        for g in range(groups):
            k_copy(g).start()

    barrier = pltpu.get_barrier_semaphore()

    @pl.when(is_live)
    def _():
        for step in range(1, n_seq):
            pl.semaphore_signal(
                barrier, inc=1, device_id={"seq": to_seq(step)}, device_id_type=MESH
            )

    for step in range(1, n_head):
        pl.semaphore_signal(
            barrier, inc=1, device_id={"head": to_head(step)}, device_id_type=MESH
        )

    for copy in staged:
        copy.start()

    def q_copy(n, to):
        return remote(qry_hbm, qall.at[me], q_send.at[n], q_recv.at[me], "seq", to)

    @pl.when(is_live)
    def _():
        pl.semaphore_wait(barrier, live - 1 + n_head - 1)
        for step in range(1, live):
            q_copy(step - 1, to_live(step)).start()

    @pl.when(jnp.logical_not(is_live))
    def _():
        pl.semaphore_wait(barrier, live + n_head - 1)
        for d in range(live):
            q_copy(d, d).start()
        for g in range(groups):
            w_copy(g).start()

    keeper = first + lax.div(me, owned)
    place = lax.rem(me, owned)

    def kv_copy(n, slot):
        ref = (key_hbm, val_hbm)[n]
        return remote(
            ref, kvown.at[slot, n], kv_send.at[n], kv_recv.at[slot, n], "seq", keeper
        )

    @pl.when(keeper != me)
    def _():
        for n in range(2):
            kv_copy(n, place).start()

    for copy in staged:
        copy.wait()

    @pl.when(keeper == me)
    def _():
        kvown[place, 0] = key_ref[...]
        kvown[place, 1] = val_ref[...]

    def lane_of(p):
        return lax.broadcasted_iota(jnp.int32, (sizes[p], hdim), 1)

    def lanes(h):
        return slice(h * hdim, (h + 1) * hdim)

    def lines(h):
        return slice(h * rows, (h + 1) * rows)

    def p_copy(p, m):
        return remote(
            sendb[p].at[m], recvb[p].at[me], p_send.at[p, m], p_recv.at[p, me], "seq", first + m
        )

    @pl.when(is_live)
    def attend():
        line = lax.broadcasted_iota(jnp.int32, (rows, 1), 0)
        begin = jnp.zeros((rows, 1), jnp.int32)
        end = jnp.zeros((rows, 1), jnp.int32)
        at = jnp.int32(0)
        for i in range(n_seq):
            after = at + seg_ref[i]
            hit = (line // 2) == row_ref[i]
            begin = jnp.where(hit, at * BLK, begin)
            end = jnp.where(hit, after * BLK, end)
            at = after
        token = me * tokens + lax.broadcasted_iota(jnp.int32, (rows, tokens), 1)
        gap = (end + lax.rem(line, 2) - token).astype(jnp.float32)
        dist[...] = jnp.where((token >= begin) & (token < end), gap, FAR)
        odd = lax.rem(lax.broadcasted_iota(jnp.int32, (rows, hdim), 1), 2) == 1

        for g in range(groups):
            k_copy(g).wait()
            if g == 0:
                for i in range(groups):
                    v_copy(i).start()
            for h in range(g * unit, (g + 1) * unit):
                kturn[lanes(h), :] = kbuf[:, lanes(h)].T
        qall[me] = qry_ref[...]
        for step in range(1, n_seq):
            source = to_seq(step)
            remote(
                qry_ref, qall.at[source], q_send.at[0], q_recv.at[source], "seq", source
            ).wait_recv()
        for r in range(n_seq):
            qx[2 * r : 2 * r + 2, :] = qall[r].astype(jnp.float32)

        def scores(h):
            dots = jnp.dot(
                qx[:, lanes(h)].astype(jnp.bfloat16),
                kturn[lanes(h), :],
                preferred_element_type=jnp.float32,
            )
            sbuf[lines(h), :] = dots * scale - slope_ref[h] * dist[...]

        def soften(h):
            score = sbuf[lines(h), :]
            top = jnp.max(score, axis=-1, keepdims=True)
            prob = jnp.exp(score - top)
            total = jnp.sum(prob, axis=-1, keepdims=True)
            pbuf[lines(h), :] = prob.astype(jnp.bfloat16)
            st2d[lines(h), :] = jnp.where(odd, total, top)

        def weigh(h):
            o2d[lines(h), :] = jnp.dot(
                pbuf[lines(h), :], vbuf[:, lanes(h)], preferred_element_type=jnp.float32
            )

        def message(p):
            base, some, lane = starts[p] * rows, sizes[p], lane_of(p)
            for m in range(mergers):
                stat = None
                for k in range(owned):
                    for s in range(2):
                        n = 2 * (m * owned + k) + s
                        x = st2d[pl.ds(base + n, some, stride=rows), :]
                        here = (lane // 16 == k) & (lax.rem(lane, 4) // 2 == s)
                        stat = x if stat is None else jnp.where(here, x, stat)
                        sendb[p][m, 2 * k + s] = o2d[
                            pl.ds(base + n, some, stride=rows), :
                        ].astype(jnp.bfloat16)
                high = stat.astype(jnp.bfloat16).astype(jnp.float32)
                rest = stat - high
                middle = rest.astype(jnp.bfloat16).astype(jnp.float32)
                low = rest - middle
                piece = lax.rem(lane, 16) // 4
                sendb[p][m, 2 * owned] = jnp.where(
                    piece == 0, high, jnp.where(piece == 1, middle, low)
                ).astype(jnp.bfloat16)

        for h in range(heads + 2 * LAG):
            if h < heads:
                scores(h)
            if 0 <= h - LAG < heads:
                soften(h - LAG)
            if 0 <= h - 2 * LAG:
                if (h - 2 * LAG) % unit == 0:
                    v_copy((h - 2 * LAG) // unit).wait()
                    w_copy((h - 2 * LAG) // unit).start()
                weigh(h - 2 * LAG)
            if h - 2 * LAG + 1 in starts[1:] + [heads]:
                p = (starts[1:] + [heads]).index(h - 2 * LAG + 1)
                message(p)
                for m in range(mergers):

                    @pl.when(me != first + m)
                    def _():
                        p_copy(p, m).start()

                    @pl.when(me == first + m)
                    def _():
                        recvb[p][me] = sendb[p][m]

    group = me - first

    def a_copy(p, to, n):
        return remote(
            xin[p].at[group], xin[p].at[group], a_send.at[p, n], a_recv.at[p, group], "seq", to
        )

    @pl.when(is_merger)
    def combine():
        base = group * owned
        for k in range(owned):

            @pl.when(base + k != me)
            def _():
                for n in range(2):
                    kv_copy(n, k).wait_recv()

        for k in range(owned):
            for n, ref in enumerate((qall.at[base + k], kvown.at[k, 0], kvown.at[k, 1])):
                for h in range(heads):
                    own2d[k, n, 2 * h : 2 * h + 2, :] = ref[:, lanes(h)].astype(jnp.float32)

        def own_terms(k, p):
            some, begin, lane = sizes[p], starts[p], lane_of(p)
            hline = lax.broadcasted_iota(jnp.int32, (some, 1), 0)
            own = [
                [own2d.at[k, n][pl.ds(2 * begin + t, some, stride=2), :] for t in range(2)]
                for n in range(3)
            ]
            slope_col = jnp.zeros((some, 1), jnp.float32)
            for h in range(some):
                slope_col = jnp.where(hline == h, slope_ref[begin + h], slope_col)
            e00 = jnp.sum(own[0][0] * own[1][0], axis=-1, keepdims=True) * scale
            e10 = jnp.sum(own[0][1] * own[1][0], axis=-1, keepdims=True) * scale - slope_col
            e11 = jnp.sum(own[0][1] * own[1][1], axis=-1, keepdims=True) * scale
            upper = jnp.maximum(e10, e11)
            w10 = jnp.exp(e10 - upper)
            w11 = jnp.exp(e11 - upper)
            j = lax.rem(lane, 4)
            stat = jnp.where(
                j == 0, e00, jnp.where(j == 1, 1.0, jnp.where(j == 2, upper, w10 + w11))
            )
            return stat, [own[2][0], w10 * own[2][0] + w11 * own[2][1]]

        own = [[own_terms(k, p) for k in range(owned)] for p in range(parts)]

        def merge(p):
            some, lane = sizes[p], lane_of(p)
            stat = own[p][0][0]
            for k in range(1, owned):
                stat = jnp.where(lane // 16 == k, own[p][k][0], stat)
            stats = [stat]
            for j in range(live):
                x = recvb[p][j, 2 * owned].astype(jnp.float32)
                x = x + pltpu.roll(x, hdim - 4, 1) + pltpu.roll(x, hdim - 8, 1)
                stats.append(x)
            highest = functools.reduce(jnp.maximum, stats)
            factors = [jnp.exp(jnp.minimum(x - highest, 0.0)) for x in stats]
            total = sum(f * pltpu.roll(x, hdim - 1, 1) for f, x in zip(factors, stats))
            inverse = 1.0 / total
            for k in range(owned):
                for s in range(2):
                    c = slice(16 * k + 2 * s, 16 * k + 2 * s + 1)
                    acc = factors[0][:, c] * own[p][k][1][s]
                    for j in range(live):
                        acc += factors[j + 1][:, c] * recvb[p][j, 2 * k + s].astype(jnp.float32)
                    n = k // per * 2 * per + s * per + k % per
                    q2d[pl.ds(n * slot, some), :] = acc * inverse[:, c]
            for h in range(some):
                xin[p][group, :, lanes(h)] = q2d[
                    pl.ds(h, 2 * owned, stride=slot), :
                ].astype(jnp.bfloat16)

        for p in range(parts):
            for step in range(1, live):
                source = to_live(step)
                remote(
                    sendb[p].at[0], recvb[p].at[source], p_send.at[p, 0], p_recv.at[p, source],
                    "seq", source,
                ).wait_recv()
            merge(p)
            for n in range(1, n_seq):
                a_copy(p, other(n - 1), n - 1).start()

    for g in range(groups):
        w_copy(g).wait()

    def h_copy(c, step):
        at = slice(c * tile, (c + 1) * tile)
        return remote(
            shares.at[to_head(step), :, at],
            got.at[step - 1, :, at],
            h_send.at[c, step - 1],
            h_recv.at[c, step - 1],
            "head",
            to_head(step),
        )

    for p in range(parts):
        for m in range(mergers):

            @pl.when(me != first + m)
            def _():
                here = xin[p].at[m]
                remote(
                    here, here, a_send.at[p, 0], a_recv.at[p, m], "seq", first + m
                ).wait_recv()

        x = jnp.concatenate([xin[p][m] for m in range(mergers)], axis=0)
        deep = slice(starts[p] * hdim, (starts[p] + sizes[p]) * hdim)
        for c in range(cols // tile):
            at = slice(c * tile, (c + 1) * tile)
            part = jnp.dot(x, wbuf[deep, at], preferred_element_type=jnp.float32)
            if p > 0:
                part += sofar[:, at]
            if p < parts - 1:
                sofar[:, at] = part
                continue
            for k in range(n_head):
                shares[k, :, at] = part[2 * per * k : 2 * per * (k + 1)].astype(jnp.bfloat16)
            for step in range(1, n_head):
                h_copy(c, step).start()

    summed = shares[mine].astype(jnp.float32)
    for step in range(1, n_head):
        for c in range(cols // tile):
            h_copy(c, step).wait_recv()
        summed += got[step - 1].astype(jnp.float32)
    for s in range(2):
        out_ref[s] = (
            res_ref[s].astype(jnp.float32) + summed[s * per : (s + 1) * per]
        ).astype(jnp.bfloat16)

    @pl.when(is_live)
    def _():
        for step in range(1, live):
            q_copy(step - 1, to_live(step)).wait_send()
        for m in range(mergers):

            @pl.when(me != first + m)
            def _():
                for p in range(parts):
                    p_copy(p, m).wait_send()

    @pl.when(jnp.logical_not(is_live))
    def _():
        for d in range(live):
            q_copy(d, d).wait_send()

    @pl.when(keeper != me)
    def _():
        for n in range(2):
            kv_copy(n, place).wait_send()

    @pl.when(is_merger)
    def _():
        for p in range(parts):
            for n in range(1, n_seq):
                a_copy(p, other(n - 1), n - 1).wait_send()

    for step in range(1, n_head):
        for c in range(cols // tile):
            h_copy(c, step).wait_send()


def body(
    n_seq,
    n_head,
    queries,
    new_keys,
    new_values,
    cache_keys,
    cache_values,
    slopes,
    seg_blocks,
    request_row,
    out_weight,
    residual,
):
    heads = slopes.shape[0]
    width = queries.shape[2]
    hdim = width // heads
    tokens = cache_keys.shape[0]
    cols = out_weight.shape[1]
    assert queries.shape[1] == 1 and seg_blocks.shape[0] == n_seq
    flat = [x.reshape(2, width) for x in (queries, new_keys, new_values)]
    unit = heads // 2
    tile = cols
    rows = 2 * n_seq
    per = n_seq // n_head
    sizes = (heads * 3 // 7, heads * 2 // 7, heads * 2 // 7)
    parts = len(sizes)
    slot = -(-max(sizes) // 8) * 8
    live, first, mergers = 3 * n_seq // 4, 0, n_head
    owned = n_seq // mergers
    assert n_seq % 4 == 0 and owned % per == 0 and 16 * owned <= hdim
    assert sum(sizes) == heads
    groups = heads // unit
    bf16, f32 = jnp.bfloat16, jnp.float32
    dma = pltpu.SemaphoreType.DMA
    vmem = pl.BlockSpec(memory_space=pltpu.VMEM)
    hbm = pl.BlockSpec(memory_space=pl.ANY)
    return pl.pallas_call(
        functools.partial(kernel, n_seq, n_head, heads, unit, tile, live, first, mergers, sizes),
        out_shape=jax.ShapeDtypeStruct(residual.shape, residual.dtype),
        in_specs=[hbm] * 10,
        out_specs=vmem,
        scratch_shapes=[
            pltpu.VMEM((2, width), bf16),
            pltpu.VMEM((2, width), bf16),
            pltpu.VMEM((2, width), bf16),
            pltpu.SMEM(seg_blocks.shape, jnp.int32),
            pltpu.SMEM(request_row.shape, jnp.int32),
            pltpu.SMEM(slopes.shape, f32),
            pltpu.VMEM(residual.shape, bf16),
            dma((7,)),
            pltpu.VMEM(cache_keys.shape, bf16),
            pltpu.VMEM((width, tokens), bf16),
            pltpu.VMEM(cache_values.shape, bf16),
            pltpu.VMEM(out_weight.shape, bf16),
            pltpu.VMEM((n_seq, 2, width), bf16),
            pltpu.VMEM((owned, 2, 2, width), bf16),
            pltpu.VMEM((owned, 3, 2 * heads, hdim), f32),
            pltpu.VMEM((rows, width), f32),
            pltpu.VMEM((heads * rows, tokens), f32),
            pltpu.VMEM((heads * rows, tokens), bf16),
            pltpu.VMEM((2 * owned * slot, hdim), f32),
            pltpu.VMEM((rows, tokens), f32),
            pltpu.VMEM((heads * rows, hdim), f32),
            pltpu.VMEM((heads * rows, hdim), f32),
            tuple(pltpu.VMEM((mergers, 2 * owned + 1, n, hdim), bf16) for n in sizes),
            tuple(pltpu.VMEM((live, 2 * owned + 1, n, hdim), bf16) for n in sizes),
            tuple(pltpu.VMEM((mergers, 2 * owned, n * hdim), bf16) for n in sizes),
            pltpu.VMEM((rows, cols), f32),
            pltpu.VMEM((n_head, 2 * per, cols), bf16),
            pltpu.VMEM((n_head - 1, 2 * per, cols), bf16),
            dma((groups,)),
            dma((groups,)),
            dma((groups,)),
            dma((live,)),
            dma((n_seq,)),
            dma((2,)),
            dma((owned, 2)),
            dma((parts, mergers)),
            dma((parts, live)),
            dma((parts, n_seq - 1)),
            dma((parts, mergers)),
            dma((cols // tile, n_head - 1)),
            dma((cols // tile, n_head - 1)),
        ],
        compiler_params=pltpu.CompilerParams(
            collective_id=0, has_side_effects=True, vmem_limit_bytes=56 << 20
        ),
    )(*flat, seg_blocks, request_row, slopes, residual, cache_keys, cache_values, out_weight)


def solution(mesh):
    in_specs = (
        P(None, "seq", "head"),
        P(None, "seq", "head"),
        P(None, "seq", "head"),
        P("seq", "head"),
        P("seq", "head"),
        P("head"),
        P(),
        P(),
        P("head", "seq"),
        P(None, "head", "seq"),
    )
    out_specs = P(None, "head", "seq")
    sizes = (mesh.shape["seq"], mesh.shape["head"])
    return jax.shard_map(
        functools.partial(body, *sizes),
        mesh=mesh,
        in_specs=in_specs,
        out_specs=out_specs,
        check_vma=False,
    )
```

```python
import functools
import math

import jax
import jax.numpy as jnp
from jax import lax
from jax.experimental import pallas as pl
from jax.experimental.pallas import tpu as pltpu
from jax.sharding import PartitionSpec as P

BLK = 128
FAR = 1e35
LAG = 3
MESH = pl.DeviceIdType.MESH


def kernel(
    n_seq,
    n_head,
    heads,
    unit,
    tile,
    live,
    first,
    mergers,
    sizes,
    qry_hbm,
    key_hbm,
    val_hbm,
    seg_hbm,
    row_hbm,
    slope_hbm,
    res_hbm,
    k_hbm,
    v_hbm,
    w_hbm,
    out_ref,
    qry_ref,
    key_ref,
    val_ref,
    seg_ref,
    row_ref,
    slope_ref,
    res_ref,
    i_sem,
    kbuf,
    kturn,
    vbuf,
    wbuf,
    qall,
    kvown,
    own2d,
    qx,
    sbuf,
    pbuf,
    q2d,
    dist,
    o2d,
    st2d,
    sendb,
    recvb,
    xin,
    sofar,
    shares,
    got,
    k_sem,
    v_sem,
    w_sem,
    q_send,
    q_recv,
    kv_send,
    kv_recv,
    p_send,
    p_recv,
    a_send,
    a_recv,
    h_send,
    h_recv,
):
    hdim = qry_ref.shape[1] // heads
    rows = 2 * n_seq
    per = n_seq // n_head
    owned = n_seq // mergers
    tokens = k_hbm.shape[0]
    groups = heads // unit
    parts = len(sizes)
    starts = [sum(sizes[:p]) for p in range(parts)]
    slot = q2d.shape[0] // (2 * owned)
    wide = unit * hdim
    cols = w_hbm.shape[1]
    scale = 1.0 / math.sqrt(hdim)
    me = lax.axis_index("seq")
    mine = lax.axis_index("head")
    is_live = me < live
    is_merger = (me >= first) & (me < first + mergers)

    def k_copy(g):
        at = pl.ds(pl.multiple_of(g * wide, 128), wide)
        return pltpu.make_async_copy(k_hbm.at[:, at], kbuf.at[:, at], k_sem.at[g])

    def v_copy(g):
        at = pl.ds(pl.multiple_of(g * wide, 128), wide)
        return pltpu.make_async_copy(v_hbm.at[:, at], vbuf.at[:, at], v_sem.at[g])

    def w_copy(g):
        at = pl.ds(pl.multiple_of(g * wide, 128), wide)
        return pltpu.make_async_copy(w_hbm.at[at], wbuf.at[at], w_sem.at[g])

    staged = [
        pltpu.make_async_copy(src, dst, i_sem.at[n])
        for n, (src, dst) in enumerate(
            (
                (qry_hbm, qry_ref),
                (key_hbm, key_ref),
                (val_hbm, val_ref),
                (seg_hbm, seg_ref),
                (row_hbm, row_ref),
                (slope_hbm, slope_ref),
                (res_hbm, res_ref),
            )
        )
    ]

    def to_seq(step):
        return lax.rem(me + step, n_seq)

    def to_live(step):
        return lax.rem(me + step, live)

    def other(n):
        return n + jnp.where(me <= n, 1, 0)

    def to_head(step):
        return lax.rem(mine + step, n_head)

    def remote(src, dst, send, recv, axis, to):
        return pltpu.make_async_remote_copy(
            src_ref=src,
            dst_ref=dst,
            send_sem=send,
            recv_sem=recv,
            device_id={axis: to},
            device_id_type=MESH,
        )

    @pl.when(is_live)
    def _():
        for g in range(groups):
            k_copy(g).start()

    barrier = pltpu.get_barrier_semaphore()

    @pl.when(is_live)
    def _():
        for step in range(1, n_seq):
            pl.semaphore_signal(
                barrier, inc=1, device_id={"seq": to_seq(step)}, device_id_type=MESH
            )

    for step in range(1, n_head):
        pl.semaphore_signal(
            barrier, inc=1, device_id={"head": to_head(step)}, device_id_type=MESH
        )

    for copy in staged:
        copy.start()

    def q_copy(n, to):
        return remote(qry_hbm, qall.at[me], q_send.at[n], q_recv.at[me], "seq", to)

    @pl.when(is_live)
    def _():
        pl.semaphore_wait(barrier, live - 1 + n_head - 1)
        for step in range(1, live):
            q_copy(step - 1, to_live(step)).start()

    @pl.when(jnp.logical_not(is_live))
    def _():
        pl.semaphore_wait(barrier, live + n_head - 1)
        for d in range(live):
            q_copy(d, d).start()
        for g in range(groups):
            w_copy(g).start()

    keeper = first + lax.div(me, owned)
    place = lax.rem(me, owned)

    def kv_copy(n, slot):
        ref = (key_hbm, val_hbm)[n]
        return remote(
            ref, kvown.at[slot, n], kv_send.at[n], kv_recv.at[slot, n], "seq", keeper
        )

    @pl.when(keeper != me)
    def _():
        for n in range(2):
            kv_copy(n, place).start()

    for copy in staged:
        copy.wait()

    @pl.when(keeper == me)
    def _():
        kvown[place, 0] = key_ref[...]
        kvown[place, 1] = val_ref[...]

    def lane_of(p):
        return lax.broadcasted_iota(jnp.int32, (sizes[p], hdim), 1)

    def lanes(h):
        return slice(h * hdim, (h + 1) * hdim)

    def lines(h):
        return slice(h * rows, (h + 1) * rows)

    def p_copy(p, m):
        return remote(
            sendb[p].at[m], recvb[p].at[me], p_send.at[p, m], p_recv.at[p, me], "seq", first + m
        )

    @pl.when(is_live)
    def attend():
        line = lax.broadcasted_iota(jnp.int32, (rows, 1), 0)
        begin = jnp.zeros((rows, 1), jnp.int32)
        end = jnp.zeros((rows, 1), jnp.int32)
        at = jnp.int32(0)
        for i in range(n_seq):
            after = at + seg_ref[i]
            hit = (line // 2) == row_ref[i]
            begin = jnp.where(hit, at * BLK, begin)
            end = jnp.where(hit, after * BLK, end)
            at = after
        token = me * tokens + lax.broadcasted_iota(jnp.int32, (rows, tokens), 1)
        gap = (end + lax.rem(line, 2) - token).astype(jnp.float32)
        dist[...] = jnp.where((token >= begin) & (token < end), gap, FAR)
        odd = lax.rem(lax.broadcasted_iota(jnp.int32, (rows, hdim), 1), 2) == 1

        for g in range(groups):
            k_copy(g).wait()
            if g == 0:
                for i in range(groups):
                    v_copy(i).start()
            for h in range(g * unit, (g + 1) * unit):
                kturn[lanes(h), :] = kbuf[:, lanes(h)].T
        qall[me] = qry_ref[...]
        for step in range(1, n_seq):
            source = to_seq(step)
            remote(
                qry_ref, qall.at[source], q_send.at[0], q_recv.at[source], "seq", source
            ).wait_recv()
        for r in range(n_seq):
            qx[2 * r : 2 * r + 2, :] = qall[r].astype(jnp.float32)

        def scores(h):
            dots = jnp.dot(
                qx[:, lanes(h)].astype(jnp.bfloat16),
                kturn[lanes(h), :],
                preferred_element_type=jnp.float32,
            )
            sbuf[lines(h), :] = dots * scale - slope_ref[h] * dist[...]

        def soften(h):
            score = sbuf[lines(h), :]
            top = jnp.max(score, axis=-1, keepdims=True)
            prob = jnp.exp(score - top)
            total = jnp.sum(prob, axis=-1, keepdims=True)
            pbuf[lines(h), :] = prob.astype(jnp.bfloat16)
            st2d[lines(h), :] = jnp.where(odd, total, top)

        def weigh(h):
            o2d[lines(h), :] = jnp.dot(
                pbuf[lines(h), :], vbuf[:, lanes(h)], preferred_element_type=jnp.float32
            )

        def message(p, m):
            base, some, lane = starts[p] * rows, sizes[p], lane_of(p)
            stat = None
            for k in range(owned):
                for s in range(2):
                    n = 2 * (m * owned + k) + s
                    x = st2d[pl.ds(base + n, some, stride=rows), :]
                    here = (lane // 16 == k) & (lax.rem(lane, 4) // 2 == s)
                    stat = x if stat is None else jnp.where(here, x, stat)
                    sendb[p][m, 2 * k + s] = o2d[
                        pl.ds(base + n, some, stride=rows), :
                    ].astype(jnp.bfloat16)
            high = stat.astype(jnp.bfloat16).astype(jnp.float32)
            rest = stat - high
            middle = rest.astype(jnp.bfloat16).astype(jnp.float32)
            low = rest - middle
            piece = lax.rem(lane, 16) // 4
            sendb[p][m, 2 * owned] = jnp.where(
                piece == 0, high, jnp.where(piece == 1, middle, low)
            ).astype(jnp.bfloat16)

        for h in range(heads + 2 * LAG):
            if h < heads:
                scores(h)
            if 0 <= h - LAG < heads:
                soften(h - LAG)
            if 0 <= h - 2 * LAG:
                if (h - 2 * LAG) % unit == 0:
                    v_copy((h - 2 * LAG) // unit).wait()
                    w_copy((h - 2 * LAG) // unit).start()
                weigh(h - 2 * LAG)
            if h - 2 * LAG + 1 in starts[1:] + [heads]:
                p = (starts[1:] + [heads]).index(h - 2 * LAG + 1)
                for m in reversed(range(mergers)):
                    message(p, m)

                    @pl.when(me != first + m)
                    def _():
                        p_copy(p, m).start()

                    @pl.when(me == first + m)
                    def _():
                        recvb[p][me] = sendb[p][m]

    group = me - first

    def a_copy(p, to, n):
        return remote(
            xin[p].at[group], xin[p].at[group], a_send.at[p, n], a_recv.at[p, group], "seq", to
        )

    @pl.when(is_merger)
    def combine():
        base = group * owned
        for k in range(owned):

            @pl.when(base + k != me)
            def _():
                for n in range(2):
                    kv_copy(n, k).wait_recv()

        for k in range(owned):
            for n, ref in enumerate((qall.at[base + k], kvown.at[k, 0], kvown.at[k, 1])):
                for h in range(heads):
                    own2d[k, n, 2 * h : 2 * h + 2, :] = ref[:, lanes(h)].astype(jnp.float32)

        def own_terms(k, p):
            some, begin, lane = sizes[p], starts[p], lane_of(p)
            hline = lax.broadcasted_iota(jnp.int32, (some, 1), 0)
            own = [
                [own2d.at[k, n][pl.ds(2 * begin + t, some, stride=2), :] for t in range(2)]
                for n in range(3)
            ]
            slope_col = jnp.zeros((some, 1), jnp.float32)
            for h in range(some):
                slope_col = jnp.where(hline == h, slope_ref[begin + h], slope_col)
            e00 = jnp.sum(own[0][0] * own[1][0], axis=-1, keepdims=True) * scale
            e10 = jnp.sum(own[0][1] * own[1][0], axis=-1, keepdims=True) * scale - slope_col
            e11 = jnp.sum(own[0][1] * own[1][1], axis=-1, keepdims=True) * scale
            upper = jnp.maximum(e10, e11)
            w10 = jnp.exp(e10 - upper)
            w11 = jnp.exp(e11 - upper)
            j = lax.rem(lane, 4)
            stat = jnp.where(
                j == 0, e00, jnp.where(j == 1, 1.0, jnp.where(j == 2, upper, w10 + w11))
            )
            return stat, [own[2][0], w10 * own[2][0] + w11 * own[2][1]]

        own = [[own_terms(k, p) for k in range(owned)] for p in range(parts)]

        def merge(p):
            some, lane = sizes[p], lane_of(p)
            stat = own[p][0][0]
            for k in range(1, owned):
                stat = jnp.where(lane // 16 == k, own[p][k][0], stat)
            stats = [stat]
            for j in range(live):
                x = recvb[p][j, 2 * owned].astype(jnp.float32)
                x = x + pltpu.roll(x, hdim - 4, 1) + pltpu.roll(x, hdim - 8, 1)
                stats.append(x)
            highest = functools.reduce(jnp.maximum, stats)
            factors = [jnp.exp(jnp.minimum(x - highest, 0.0)) for x in stats]
            total = sum(f * pltpu.roll(x, hdim - 1, 1) for f, x in zip(factors, stats))
            inverse = 1.0 / total
            for k in range(owned):
                for s in range(2):
                    c = slice(16 * k + 2 * s, 16 * k + 2 * s + 1)
                    acc = factors[0][:, c] * own[p][k][1][s]
                    for j in range(live):
                        acc += factors[j + 1][:, c] * recvb[p][j, 2 * k + s].astype(jnp.float32)
                    n = k // per * 2 * per + s * per + k % per
                    q2d[pl.ds(n * slot, some), :] = acc * inverse[:, c]
            for h in range(some):
                xin[p][group, :, lanes(h)] = q2d[
                    pl.ds(h, 2 * owned, stride=slot), :
                ].astype(jnp.bfloat16)

        for p in range(parts):
            for step in range(1, live):
                source = to_live(step)
                remote(
                    sendb[p].at[0], recvb[p].at[source], p_send.at[p, 0], p_recv.at[p, source],
                    "seq", source,
                ).wait_recv()
            merge(p)
            for n in range(1, n_seq):
                a_copy(p, other(n - 1), n - 1).start()

    for g in range(groups):
        w_copy(g).wait()

    def h_copy(c, step):
        at = slice(c * tile, (c + 1) * tile)
        return remote(
            shares.at[to_head(step), :, at],
            got.at[step - 1, :, at],
            h_send.at[c, step - 1],
            h_recv.at[c, step - 1],
            "head",
            to_head(step),
        )

    for p in range(parts):
        for m in range(mergers):

            @pl.when(me != first + m)
            def _():
                here = xin[p].at[m]
                remote(
                    here, here, a_send.at[p, 0], a_recv.at[p, m], "seq", first + m
                ).wait_recv()

        x = jnp.concatenate([xin[p][m] for m in range(mergers)], axis=0)
        deep = slice(starts[p] * hdim, (starts[p] + sizes[p]) * hdim)
        for c in range(cols // tile):
            at = slice(c * tile, (c + 1) * tile)
            part = jnp.dot(x, wbuf[deep, at], preferred_element_type=jnp.float32)
            if p > 0:
                part += sofar[:, at]
            if p < parts - 1:
                sofar[:, at] = part
                continue
            for k in range(n_head):
                shares[k, :, at] = part[2 * per * k : 2 * per * (k + 1)].astype(jnp.bfloat16)
            for step in range(1, n_head):
                h_copy(c, step).start()

    summed = shares[mine].astype(jnp.float32)
    for step in range(1, n_head):
        for c in range(cols // tile):
            h_copy(c, step).wait_recv()
        summed += got[step - 1].astype(jnp.float32)
    for s in range(2):
        out_ref[s] = (
            res_ref[s].astype(jnp.float32) + summed[s * per : (s + 1) * per]
        ).astype(jnp.bfloat16)

    @pl.when(is_live)
    def _():
        for step in range(1, live):
            q_copy(step - 1, to_live(step)).wait_send()
        for m in range(mergers):

            @pl.when(me != first + m)
            def _():
                for p in range(parts):
                    p_copy(p, m).wait_send()

    @pl.when(jnp.logical_not(is_live))
    def _():
        for d in range(live):
            q_copy(d, d).wait_send()

    @pl.when(keeper != me)
    def _():
        for n in range(2):
            kv_copy(n, place).wait_send()

    @pl.when(is_merger)
    def _():
        for p in range(parts):
            for n in range(1, n_seq):
                a_copy(p, other(n - 1), n - 1).wait_send()

    for step in range(1, n_head):
        for c in range(cols // tile):
            h_copy(c, step).wait_send()


def body(
    n_seq,
    n_head,
    queries,
    new_keys,
    new_values,
    cache_keys,
    cache_values,
    slopes,
    seg_blocks,
    request_row,
    out_weight,
    residual,
):
    heads = slopes.shape[0]
    width = queries.shape[2]
    hdim = width // heads
    tokens = cache_keys.shape[0]
    cols = out_weight.shape[1]
    assert queries.shape[1] == 1 and seg_blocks.shape[0] == n_seq
    flat = [x.reshape(2, width) for x in (queries, new_keys, new_values)]
    unit = heads // 2
    tile = cols
    rows = 2 * n_seq
    per = n_seq // n_head
    sizes = (heads * 3 // 7, heads * 2 // 7, heads * 2 // 7)
    parts = len(sizes)
    slot = -(-max(sizes) // 8) * 8
    live, first, mergers = 3 * n_seq // 4, 0, n_head
    owned = n_seq // mergers
    assert n_seq % 4 == 0 and owned % per == 0 and 16 * owned <= hdim
    assert sum(sizes) == heads
    groups = heads // unit
    bf16, f32 = jnp.bfloat16, jnp.float32
    dma = pltpu.SemaphoreType.DMA
    vmem = pl.BlockSpec(memory_space=pltpu.VMEM)
    hbm = pl.BlockSpec(memory_space=pl.ANY)
    return pl.pallas_call(
        functools.partial(kernel, n_seq, n_head, heads, unit, tile, live, first, mergers, sizes),
        out_shape=pltpu.VMEM(residual.shape, residual.dtype),
        in_specs=[hbm] * 10,
        out_specs=vmem,
        scratch_shapes=[
            pltpu.VMEM((2, width), bf16),
            pltpu.VMEM((2, width), bf16),
            pltpu.VMEM((2, width), bf16),
            pltpu.SMEM(seg_blocks.shape, jnp.int32),
            pltpu.SMEM(request_row.shape, jnp.int32),
            pltpu.SMEM(slopes.shape, f32),
            pltpu.VMEM(residual.shape, bf16),
            dma((7,)),
            pltpu.VMEM(cache_keys.shape, bf16),
            pltpu.VMEM((width, tokens), bf16),
            pltpu.VMEM(cache_values.shape, bf16),
            pltpu.VMEM(out_weight.shape, bf16),
            pltpu.VMEM((n_seq, 2, width), bf16),
            pltpu.VMEM((owned, 2, 2, width), bf16),
            pltpu.VMEM((owned, 3, 2 * heads, hdim), f32),
            pltpu.VMEM((rows, width), f32),
            pltpu.VMEM((heads * rows, tokens), f32),
            pltpu.VMEM((heads * rows, tokens), bf16),
            pltpu.VMEM((2 * owned * slot, hdim), f32),
            pltpu.VMEM((rows, tokens), f32),
            pltpu.VMEM((heads * rows, hdim), f32),
            pltpu.VMEM((heads * rows, hdim), f32),
            tuple(pltpu.VMEM((mergers, 2 * owned + 1, n, hdim), bf16) for n in sizes),
            tuple(pltpu.VMEM((live, 2 * owned + 1, n, hdim), bf16) for n in sizes),
            tuple(pltpu.VMEM((mergers, 2 * owned, n * hdim), bf16) for n in sizes),
            pltpu.VMEM((rows, cols), f32),
            pltpu.VMEM((n_head, 2 * per, cols), bf16),
            pltpu.VMEM((n_head - 1, 2 * per, cols), bf16),
            dma((groups,)),
            dma((groups,)),
            dma((groups,)),
            dma((live,)),
            dma((n_seq,)),
            dma((2,)),
            dma((owned, 2)),
            dma((parts, mergers)),
            dma((parts, live)),
            dma((parts, n_seq - 1)),
            dma((parts, mergers)),
            dma((cols // tile, n_head - 1)),
            dma((cols // tile, n_head - 1)),
        ],
        compiler_params=pltpu.CompilerParams(
            collective_id=0, has_side_effects=True, vmem_limit_bytes=56 << 20
        ),
    )(*flat, seg_blocks, request_row, slopes, residual, cache_keys, cache_values, out_weight)


def solution(mesh):
    in_specs = (
        P(None, "seq", "head"),
        P(None, "seq", "head"),
        P(None, "seq", "head"),
        P("seq", "head"),
        P("seq", "head"),
        P("head"),
        P(),
        P(),
        P("head", "seq"),
        P(None, "head", "seq"),
    )
    out_specs = P(None, "head", "seq")
    sizes = (mesh.shape["seq"], mesh.shape["head"])
    return jax.shard_map(
        functools.partial(body, *sizes),
        mesh=mesh,
        in_specs=in_specs,
        out_specs=out_specs,
        check_vma=False,
    )
```

```python
import functools
import math

import jax
import jax.numpy as jnp
from jax import lax
from jax.experimental import pallas as pl
from jax.experimental.pallas import tpu as pltpu
from jax.sharding import PartitionSpec as P

BLK = 128
FAR = 1e35
LAG = 3
MESH = pl.DeviceIdType.MESH


def kernel(
    n_seq,
    n_head,
    heads,
    unit,
    tile,
    live,
    first,
    mergers,
    sizes,
    qry_hbm,
    key_hbm,
    val_hbm,
    seg_hbm,
    row_hbm,
    slope_hbm,
    res_hbm,
    k_hbm,
    v_hbm,
    w_hbm,
    out_ref,
    qry_ref,
    key_ref,
    val_ref,
    seg_ref,
    row_ref,
    slope_ref,
    res_ref,
    i_sem,
    kbuf,
    kturn,
    vbuf,
    wbuf,
    qall,
    kvown,
    own2d,
    qx,
    sbuf,
    pbuf,
    q2d,
    dist,
    o2d,
    st2d,
    sendb,
    recvb,
    xin,
    sofar,
    shares,
    got,
    k_sem,
    v_sem,
    w_sem,
    q_send,
    q_recv,
    kv_send,
    kv_recv,
    p_send,
    p_recv,
    a_send,
    a_recv,
    h_send,
    h_recv,
):
    hdim = qry_ref.shape[1] // heads
    rows = 2 * n_seq
    per = n_seq // n_head
    owned = n_seq // mergers
    tokens = k_hbm.shape[0]
    groups = heads // unit
    parts = len(sizes)
    starts = [sum(sizes[:p]) for p in range(parts)]
    slot = q2d.shape[0] // (2 * owned)
    wide = unit * hdim
    cols = w_hbm.shape[1]
    scale = 1.0 / math.sqrt(hdim)
    me = lax.axis_index("seq")
    mine = lax.axis_index("head")
    is_live = me < live
    is_merger = (me >= first) & (me < first + mergers)

    def k_copy(g):
        at = pl.ds(pl.multiple_of(g * wide, 128), wide)
        return pltpu.make_async_copy(k_hbm.at[:, at], kbuf.at[:, at], k_sem.at[g])

    def v_copy(g):
        at = pl.ds(pl.multiple_of(g * wide, 128), wide)
        return pltpu.make_async_copy(v_hbm.at[:, at], vbuf.at[:, at], v_sem.at[g])

    def w_copy(g):
        at = pl.ds(pl.multiple_of(g * wide, 128), wide)
        return pltpu.make_async_copy(w_hbm.at[at], wbuf.at[at], w_sem.at[g])

    staged = [
        pltpu.make_async_copy(src, dst, i_sem.at[n])
        for n, (src, dst) in enumerate(
            (
                (qry_hbm, qry_ref),
                (key_hbm, key_ref),
                (val_hbm, val_ref),
                (seg_hbm, seg_ref),
                (row_hbm, row_ref),
                (slope_hbm, slope_ref),
                (res_hbm, res_ref),
            )
        )
    ]

    def to_seq(step):
        return lax.rem(me + step, n_seq)

    def to_live(step):
        return lax.rem(me + step, live)

    def other(n):
        return n + jnp.where(me <= n, 1, 0)

    def to_head(step):
        return lax.rem(mine + step, n_head)

    def remote(src, dst, send, recv, axis, to):
        return pltpu.make_async_remote_copy(
            src_ref=src,
            dst_ref=dst,
            send_sem=send,
            recv_sem=recv,
            device_id={axis: to},
            device_id_type=MESH,
        )

    @pl.when(is_live)
    def _():
        for g in range(groups):
            k_copy(g).start()

    barrier = pltpu.get_barrier_semaphore()

    @pl.when(is_live)
    def _():
        for step in range(1, n_seq):
            pl.semaphore_signal(
                barrier, inc=1, device_id={"seq": to_seq(step)}, device_id_type=MESH
            )

    for step in range(1, n_head):
        pl.semaphore_signal(
            barrier, inc=1, device_id={"head": to_head(step)}, device_id_type=MESH
        )

    for copy in staged:
        copy.start()

    def q_copy(n, to):
        return remote(qry_hbm, qall.at[me], q_send.at[n], q_recv.at[me], "seq", to)

    @pl.when(is_live)
    def _():
        pl.semaphore_wait(barrier, live - 1 + n_head - 1)
        for step in range(1, live):
            q_copy(step - 1, to_live(step)).start()

    @pl.when(jnp.logical_not(is_live))
    def _():
        pl.semaphore_wait(barrier, live + n_head - 1)
        for d in range(live):
            q_copy(d, d).start()
        for g in range(groups):
            w_copy(g).start()

    keeper = first + lax.div(me, owned)
    place = lax.rem(me, owned)

    def kv_copy(n, slot):
        ref = (key_hbm, val_hbm)[n]
        return remote(
            ref, kvown.at[slot, n], kv_send.at[n], kv_recv.at[slot, n], "seq", keeper
        )

    @pl.when(keeper != me)
    def _():
        for n in range(2):
            kv_copy(n, place).start()

    for copy in staged:
        copy.wait()

    @pl.when(keeper == me)
    def _():
        kvown[place, 0] = key_ref[...]
        kvown[place, 1] = val_ref[...]

    def lane_of(p):
        return lax.broadcasted_iota(jnp.int32, (sizes[p], hdim), 1)

    def lanes(h):
        return slice(h * hdim, (h + 1) * hdim)

    def lines(h):
        return slice(h * rows, (h + 1) * rows)

    def p_copy(p, m):
        return remote(
            sendb[p].at[m], recvb[p].at[me], p_send.at[p, m], p_recv.at[p, me], "seq", first + m
        )

    @pl.when(is_live)
    def attend():
        line = lax.broadcasted_iota(jnp.int32, (rows, 1), 0)
        begin = jnp.zeros((rows, 1), jnp.int32)
        end = jnp.zeros((rows, 1), jnp.int32)
        at = jnp.int32(0)
        for i in range(n_seq):
            after = at + seg_ref[i]
            hit = (line // 2) == row_ref[i]
            begin = jnp.where(hit, at * BLK, begin)
            end = jnp.where(hit, after * BLK, end)
            at = after
        token = me * tokens + lax.broadcasted_iota(jnp.int32, (rows, tokens), 1)
        gap = (end + lax.rem(line, 2) - token).astype(jnp.float32)
        dist[...] = jnp.where((token >= begin) & (token < end), gap, FAR)
        odd = lax.rem(lax.broadcasted_iota(jnp.int32, (rows, hdim), 1), 2) == 1

        for g in range(groups):
            k_copy(g).wait()
            if g == 0:
                for i in range(groups):
                    v_copy(i).start()
            for h in range(g * unit, (g + 1) * unit):
                kturn[lanes(h), :] = kbuf[:, lanes(h)].T
        qall[me] = qry_ref[...]
        for step in range(1, n_seq):
            source = to_seq(step)
            remote(
                qry_ref, qall.at[source], q_send.at[0], q_recv.at[source], "seq", source
            ).wait_recv()
        for r in range(n_seq):
            qx[2 * r : 2 * r + 2, :] = qall[r].astype(jnp.float32)

        def scores(h):
            dots = jnp.dot(
                qx[:, lanes(h)].astype(jnp.bfloat16),
                kturn[lanes(h), :],
                preferred_element_type=jnp.float32,
            )
            sbuf[lines(h), :] = dots * scale - slope_ref[h] * dist[...]

        def soften(h):
            score = sbuf[lines(h), :]
            top = jnp.max(score, axis=-1, keepdims=True)
            prob = jnp.exp(score - top)
            total = jnp.sum(prob, axis=-1, keepdims=True)
            pbuf[lines(h), :] = prob.astype(jnp.bfloat16)
            st2d[lines(h), :] = jnp.where(odd, total, top)

        def weigh(h):
            o2d[lines(h), :] = jnp.dot(
                pbuf[lines(h), :], vbuf[:, lanes(h)], preferred_element_type=jnp.float32
            )

        def message(p, m):
            base, some, lane = starts[p] * rows, sizes[p], lane_of(p)
            stat = None
            for k in range(owned):
                for s in range(2):
                    n = 2 * (m * owned + k) + s
                    x = st2d[pl.ds(base + n, some, stride=rows), :]
                    here = (lane // 16 == k) & (lax.rem(lane, 4) // 2 == s)
                    stat = x if stat is None else jnp.where(here, x, stat)
                    sendb[p][m, 2 * k + s] = o2d[
                        pl.ds(base + n, some, stride=rows), :
                    ].astype(jnp.bfloat16)
            high = stat.astype(jnp.bfloat16).astype(jnp.float32)
            rest = stat - high
            middle = rest.astype(jnp.bfloat16).astype(jnp.float32)
            low = rest - middle
            piece = lax.rem(lane, 16) // 4
            sendb[p][m, 2 * owned] = jnp.where(
                piece == 0, high, jnp.where(piece == 1, middle, low)
            ).astype(jnp.bfloat16)

        for h in range(heads + 2 * LAG):
            if h < heads:
                scores(h)
            if 0 <= h - LAG < heads:
                soften(h - LAG)
            if 0 <= h - 2 * LAG:
                if (h - 2 * LAG) % unit == 0:
                    v_copy((h - 2 * LAG) // unit).wait()
                    w_copy((h - 2 * LAG) // unit).start()
                weigh(h - 2 * LAG)
            if h - 2 * LAG + 1 in starts[1:] + [heads]:
                p = (starts[1:] + [heads]).index(h - 2 * LAG + 1)
                for m in reversed(range(mergers)):
                    message(p, m)

                    @pl.when(me != first + m)
                    def _():
                        p_copy(p, m).start()

                    @pl.when(me == first + m)
                    def _():
                        recvb[p][me] = sendb[p][m]

    group = me - first

    def a_copy(p, to, n):
        return remote(
            xin[p].at[group], xin[p].at[group], a_send.at[p, n], a_recv.at[p, group], "seq", to
        )

    @pl.when(is_merger)
    def combine():
        base = group * owned
        for k in range(owned):

            @pl.when(base + k != me)
            def _():
                for n in range(2):
                    kv_copy(n, k).wait_recv()

        for k in range(owned):
            for n, ref in enumerate((qall.at[base + k], kvown.at[k, 0], kvown.at[k, 1])):
                for h in range(heads):
                    own2d[k, n, 2 * h : 2 * h + 2, :] = ref[:, lanes(h)].astype(jnp.float32)

        def own_terms(k, p):
            some, begin, lane = sizes[p], starts[p], lane_of(p)
            hline = lax.broadcasted_iota(jnp.int32, (some, 1), 0)
            own = [
                [own2d.at[k, n][pl.ds(2 * begin + t, some, stride=2), :] for t in range(2)]
                for n in range(3)
            ]
            slope_col = jnp.zeros((some, 1), jnp.float32)
            for h in range(some):
                slope_col = jnp.where(hline == h, slope_ref[begin + h], slope_col)
            e00 = jnp.sum(own[0][0] * own[1][0], axis=-1, keepdims=True) * scale
            e10 = jnp.sum(own[0][1] * own[1][0], axis=-1, keepdims=True) * scale - slope_col
            e11 = jnp.sum(own[0][1] * own[1][1], axis=-1, keepdims=True) * scale
            upper = jnp.maximum(e10, e11)
            w10 = jnp.exp(e10 - upper)
            w11 = jnp.exp(e11 - upper)
            j = lax.rem(lane, 4)
            stat = jnp.where(
                j == 0, e00, jnp.where(j == 1, 1.0, jnp.where(j == 2, upper, w10 + w11))
            )
            return stat, [own[2][0], w10 * own[2][0] + w11 * own[2][1]]

        own = [[own_terms(k, p) for k in range(owned)] for p in range(parts)]

        def merge(p):
            some, lane = sizes[p], lane_of(p)
            stat = own[p][0][0]
            for k in range(1, owned):
                stat = jnp.where(lane // 16 == k, own[p][k][0], stat)
            stats = [stat]
            for j in range(live):
                x = recvb[p][j, 2 * owned].astype(jnp.float32)
                x = x + pltpu.roll(x, hdim - 4, 1) + pltpu.roll(x, hdim - 8, 1)
                stats.append(x)
            highest = functools.reduce(jnp.maximum, stats)
            factors = [jnp.exp(jnp.minimum(x - highest, 0.0)) for x in stats]
            total = sum(f * pltpu.roll(x, hdim - 1, 1) for f, x in zip(factors, stats))
            inverse = 1.0 / total
            for k in range(owned):
                for s in range(2):
                    c = slice(16 * k + 2 * s, 16 * k + 2 * s + 1)
                    acc = factors[0][:, c] * own[p][k][1][s]
                    for j in range(live):
                        acc += factors[j + 1][:, c] * recvb[p][j, 2 * k + s].astype(jnp.float32)
                    n = k // per * 2 * per + s * per + k % per
                    q2d[pl.ds(n * slot, some), :] = acc * inverse[:, c]
            for h in range(some):
                xin[p][group, :, lanes(h)] = q2d[
                    pl.ds(h, 2 * owned, stride=slot), :
                ].astype(jnp.bfloat16)

        for p in range(parts):
            for step in range(1, live):
                source = to_live(step)
                remote(
                    sendb[p].at[0], recvb[p].at[source], p_send.at[p, 0], p_recv.at[p, source],
                    "seq", source,
                ).wait_recv()
            merge(p)
            for n in range(1, n_seq):
                a_copy(p, other(n - 1), n - 1).start()

    for g in range(groups):
        w_copy(g).wait()

    def h_copy(c, step):
        at = slice(c * tile, (c + 1) * tile)
        return remote(
            shares.at[to_head(step), :, at],
            got.at[step - 1, :, at],
            h_send.at[c, step - 1],
            h_recv.at[c, step - 1],
            "head",
            to_head(step),
        )

    for p in range(parts):
        for m in range(mergers):

            @pl.when(me != first + m)
            def _():
                here = xin[p].at[m]
                remote(
                    here, here, a_send.at[p, 0], a_recv.at[p, m], "seq", first + m
                ).wait_recv()

        x = jnp.concatenate([xin[p][m] for m in range(mergers)], axis=0)
        deep = slice(starts[p] * hdim, (starts[p] + sizes[p]) * hdim)
        for c in range(cols // tile):
            at = slice(c * tile, (c + 1) * tile)
            part = jnp.dot(x, wbuf[deep, at], preferred_element_type=jnp.float32)
            if p > 0:
                part += sofar[:, at]
            if p < parts - 1:
                sofar[:, at] = part
                continue
            for k in range(n_head):
                shares[k, :, at] = part[2 * per * k : 2 * per * (k + 1)].astype(jnp.bfloat16)
            for step in range(1, n_head):
                h_copy(c, step).start()

    @pl.when(is_live)
    def _():
        for step in range(1, live):
            q_copy(step - 1, to_live(step)).wait_send()
        for m in range(mergers):

            @pl.when(me != first + m)
            def _():
                for p in range(parts):
                    p_copy(p, m).wait_send()

    @pl.when(jnp.logical_not(is_live))
    def _():
        for d in range(live):
            q_copy(d, d).wait_send()

    @pl.when(keeper != me)
    def _():
        for n in range(2):
            kv_copy(n, place).wait_send()

    @pl.when(is_merger)
    def _():
        for p in range(parts):
            for n in range(1, n_seq):
                a_copy(p, other(n - 1), n - 1).wait_send()

    summed = shares[mine].astype(jnp.float32)
    for step in range(1, n_head):
        for c in range(cols // tile):
            h_copy(c, step).wait_recv()
        summed += got[step - 1].astype(jnp.float32)
    for s in range(2):
        out_ref[s] = (
            res_ref[s].astype(jnp.float32) + summed[s * per : (s + 1) * per]
        ).astype(jnp.bfloat16)

    for step in range(1, n_head):
        for c in range(cols // tile):
            h_copy(c, step).wait_send()


def body(
    n_seq,
    n_head,
    queries,
    new_keys,
    new_values,
    cache_keys,
    cache_values,
    slopes,
    seg_blocks,
    request_row,
    out_weight,
    residual,
):
    heads = slopes.shape[0]
    width = queries.shape[2]
    hdim = width // heads
    tokens = cache_keys.shape[0]
    cols = out_weight.shape[1]
    assert queries.shape[1] == 1 and seg_blocks.shape[0] == n_seq
    flat = [x.reshape(2, width) for x in (queries, new_keys, new_values)]
    unit = heads // 2
    tile = cols
    rows = 2 * n_seq
    per = n_seq // n_head
    sizes = (heads * 3 // 7, heads * 2 // 7, heads * 2 // 7)
    parts = len(sizes)
    slot = -(-max(sizes) // 8) * 8
    live, first, mergers = 3 * n_seq // 4, 0, n_head
    owned = n_seq // mergers
    assert n_seq % 4 == 0 and owned % per == 0 and 16 * owned <= hdim
    assert sum(sizes) == heads
    groups = heads // unit
    bf16, f32 = jnp.bfloat16, jnp.float32
    dma = pltpu.SemaphoreType.DMA
    vmem = pl.BlockSpec(memory_space=pltpu.VMEM)
    hbm = pl.BlockSpec(memory_space=pl.ANY)
    return pl.pallas_call(
        functools.partial(kernel, n_seq, n_head, heads, unit, tile, live, first, mergers, sizes),
        out_shape=pltpu.VMEM(residual.shape, residual.dtype),
        in_specs=[hbm] * 10,
        out_specs=vmem,
        scratch_shapes=[
            pltpu.VMEM((2, width), bf16),
            pltpu.VMEM((2, width), bf16),
            pltpu.VMEM((2, width), bf16),
            pltpu.SMEM(seg_blocks.shape, jnp.int32),
            pltpu.SMEM(request_row.shape, jnp.int32),
            pltpu.SMEM(slopes.shape, f32),
            pltpu.VMEM(residual.shape, bf16),
            dma((7,)),
            pltpu.VMEM(cache_keys.shape, bf16),
            pltpu.VMEM((width, tokens), bf16),
            pltpu.VMEM(cache_values.shape, bf16),
            pltpu.VMEM(out_weight.shape, bf16),
            pltpu.VMEM((n_seq, 2, width), bf16),
            pltpu.VMEM((owned, 2, 2, width), bf16),
            pltpu.VMEM((owned, 3, 2 * heads, hdim), f32),
            pltpu.VMEM((rows, width), f32),
            pltpu.VMEM((heads * rows, tokens), f32),
            pltpu.VMEM((heads * rows, tokens), bf16),
            pltpu.VMEM((2 * owned * slot, hdim), f32),
            pltpu.VMEM((rows, tokens), f32),
            pltpu.VMEM((heads * rows, hdim), f32),
            pltpu.VMEM((heads * rows, hdim), f32),
            tuple(pltpu.VMEM((mergers, 2 * owned + 1, n, hdim), bf16) for n in sizes),
            tuple(pltpu.VMEM((live, 2 * owned + 1, n, hdim), bf16) for n in sizes),
            tuple(pltpu.VMEM((mergers, 2 * owned, n * hdim), bf16) for n in sizes),
            pltpu.VMEM((rows, cols), f32),
            pltpu.VMEM((n_head, 2 * per, cols), bf16),
            pltpu.VMEM((n_head - 1, 2 * per, cols), bf16),
            dma((groups,)),
            dma((groups,)),
            dma((groups,)),
            dma((live,)),
            dma((n_seq,)),
            dma((2,)),
            dma((owned, 2)),
            dma((parts, mergers)),
            dma((parts, live)),
            dma((parts, n_seq - 1)),
            dma((parts, mergers)),
            dma((cols // tile, n_head - 1)),
            dma((cols // tile, n_head - 1)),
        ],
        compiler_params=pltpu.CompilerParams(
            collective_id=0, has_side_effects=True, vmem_limit_bytes=56 << 20
        ),
    )(*flat, seg_blocks, request_row, slopes, residual, cache_keys, cache_values, out_weight)


def solution(mesh):
    in_specs = (
        P(None, "seq", "head"),
        P(None, "seq", "head"),
        P(None, "seq", "head"),
        P("seq", "head"),
        P("seq", "head"),
        P("head"),
        P(),
        P(),
        P("head", "seq"),
        P(None, "head", "seq"),
    )
    out_specs = P(None, "head", "seq")
    sizes = (mesh.shape["seq"], mesh.shape["head"])
    return jax.shard_map(
        functools.partial(body, *sizes),
        mesh=mesh,
        in_specs=in_specs,
        out_specs=out_specs,
        check_vma=False,
    )
```

```python
import functools
import math

import jax
import jax.numpy as jnp
from jax import lax
from jax.experimental import pallas as pl
from jax.experimental.pallas import tpu as pltpu
from jax.sharding import PartitionSpec as P

BLK = 128
FAR = 1e35
LAG = 3
MESH = pl.DeviceIdType.MESH


def kernel(
    n_seq,
    n_head,
    heads,
    unit,
    tile,
    live,
    first,
    mergers,
    sizes,
    qry_hbm,
    key_hbm,
    val_hbm,
    seg_hbm,
    row_hbm,
    slope_hbm,
    res_hbm,
    k_hbm,
    v_hbm,
    w_hbm,
    out_ref,
    qry_ref,
    key_ref,
    val_ref,
    seg_ref,
    row_ref,
    slope_ref,
    res_ref,
    i_sem,
    kbuf,
    kturn,
    vbuf,
    wbuf,
    qall,
    kvown,
    own2d,
    qx,
    sbuf,
    pbuf,
    q2d,
    dist,
    o2d,
    st2d,
    sendb,
    recvb,
    xin,
    sofar,
    shares,
    got,
    k_sem,
    v_sem,
    w_sem,
    q_send,
    q_recv,
    kv_send,
    kv_recv,
    p_send,
    p_recv,
    a_send,
    a_recv,
    h_send,
    h_recv,
):
    hdim = qry_ref.shape[1] // heads
    rows = 2 * n_seq
    per = n_seq // n_head
    owned = n_seq // mergers
    tokens = k_hbm.shape[0]
    groups = heads // unit
    parts = len(sizes)
    starts = [sum(sizes[:p]) for p in range(parts)]
    slot = q2d.shape[0] // (2 * owned)
    wide = unit * hdim
    cols = w_hbm.shape[1]
    scale = 1.0 / math.sqrt(hdim)
    me = lax.axis_index("seq")
    mine = lax.axis_index("head")
    is_live = me < live
    is_merger = (me >= first) & (me < first + mergers)

    def k_copy(g):
        at = pl.ds(pl.multiple_of(g * wide, 128), wide)
        return pltpu.make_async_copy(k_hbm.at[:, at], kbuf.at[:, at], k_sem.at[g])

    def v_copy(g):
        at = pl.ds(pl.multiple_of(g * wide, 128), wide)
        return pltpu.make_async_copy(v_hbm.at[:, at], vbuf.at[:, at], v_sem.at[g])

    def w_copy(g):
        at = pl.ds(pl.multiple_of(g * wide, 128), wide)
        return pltpu.make_async_copy(w_hbm.at[at], wbuf.at[at], w_sem.at[g])

    staged = [
        pltpu.make_async_copy(src, dst, i_sem.at[n])
        for n, (src, dst) in enumerate(
            (
                (qry_hbm, qry_ref),
                (key_hbm, key_ref),
                (val_hbm, val_ref),
                (seg_hbm, seg_ref),
                (row_hbm, row_ref),
                (slope_hbm, slope_ref),
                (res_hbm, res_ref),
            )
        )
    ]

    def to_seq(step):
        return lax.rem(me + step, n_seq)

    def to_live(step):
        return lax.rem(me + step, live)

    def other(n):
        return n + jnp.where(me <= n, 1, 0)

    def to_head(step):
        return lax.rem(mine + step, n_head)

    def remote(src, dst, send, recv, axis, to):
        return pltpu.make_async_remote_copy(
            src_ref=src,
            dst_ref=dst,
            send_sem=send,
            recv_sem=recv,
            device_id={axis: to},
            device_id_type=MESH,
        )

    @pl.when(is_live)
    def _():
        for g in range(groups):
            k_copy(g).start()

    barrier = pltpu.get_barrier_semaphore()

    @pl.when(is_live)
    def _():
        for step in range(1, n_seq):
            pl.semaphore_signal(
                barrier, inc=1, device_id={"seq": to_seq(step)}, device_id_type=MESH
            )

    for step in range(1, n_head):
        pl.semaphore_signal(
            barrier, inc=1, device_id={"head": to_head(step)}, device_id_type=MESH
        )

    for copy in staged:
        copy.start()

    def q_copy(n, to):
        return remote(qry_hbm, qall.at[me], q_send.at[n], q_recv.at[me], "seq", to)

    @pl.when(is_live)
    def _():
        pl.semaphore_wait(barrier, live - 1 + n_head - 1)
        for step in range(1, live):
            q_copy(step - 1, to_live(step)).start()

    @pl.when(jnp.logical_not(is_live))
    def _():
        pl.semaphore_wait(barrier, live + n_head - 1)
        for d in range(live):
            q_copy(d, d).start()
        for g in range(groups):
            w_copy(g).start()

    keeper = first + lax.div(me, owned)
    place = lax.rem(me, owned)

    def kv_copy(n, slot):
        ref = (key_hbm, val_hbm)[n]
        return remote(
            ref, kvown.at[slot, n], kv_send.at[n], kv_recv.at[slot, n], "seq", keeper
        )

    @pl.when(keeper != me)
    def _():
        for n in range(2):
            kv_copy(n, place).start()

    for copy in staged:
        copy.wait()

    @pl.when(keeper == me)
    def _():
        kvown[place, 0] = key_ref[...]
        kvown[place, 1] = val_ref[...]

    def lane_of(p):
        return lax.broadcasted_iota(jnp.int32, (sizes[p], hdim), 1)

    def lanes(h):
        return slice(h * hdim, (h + 1) * hdim)

    def lines(h):
        return slice(h * rows, (h + 1) * rows)

    def p_copy(p, m):
        return remote(
            sendb[p].at[m], recvb[p].at[me], p_send.at[p, m], p_recv.at[p, me], "seq", first + m
        )

    @pl.when(is_live)
    def attend():
        line = lax.broadcasted_iota(jnp.int32, (rows, 1), 0)
        begin = jnp.zeros((rows, 1), jnp.int32)
        end = jnp.zeros((rows, 1), jnp.int32)
        at = jnp.int32(0)
        for i in range(n_seq):
            after = at + seg_ref[i]
            hit = (line // 2) == row_ref[i]
            begin = jnp.where(hit, at * BLK, begin)
            end = jnp.where(hit, after * BLK, end)
            at = after
        token = me * tokens + lax.broadcasted_iota(jnp.int32, (rows, tokens), 1)
        gap = (end + lax.rem(line, 2) - token).astype(jnp.float32)
        dist[...] = jnp.where((token >= begin) & (token < end), gap, FAR)
        odd = lax.rem(lax.broadcasted_iota(jnp.int32, (rows, hdim), 1), 2) == 1

        for g in range(groups):
            k_copy(g).wait()
            if g == 0:
                for i in range(groups):
                    v_copy(i).start()
            for h in range(g * unit, (g + 1) * unit):
                kturn[lanes(h), :] = kbuf[:, lanes(h)].T
        qall[me] = qry_ref[...]
        for step in range(1, n_seq):
            source = to_seq(step)
            remote(
                qry_ref, qall.at[source], q_send.at[0], q_recv.at[source], "seq", source
            ).wait_recv()
        for r in range(n_seq):
            qx[2 * r : 2 * r + 2, :] = qall[r].astype(jnp.float32)

        def scores(h):
            dots = jnp.dot(
                qx[:, lanes(h)].astype(jnp.bfloat16),
                kturn[lanes(h), :],
                preferred_element_type=jnp.float32,
            )
            sbuf[lines(h), :] = dots * scale - slope_ref[h] * dist[...]

        def soften(h):
            score = sbuf[lines(h), :]
            top = jnp.max(score, axis=-1, keepdims=True)
            prob = jnp.exp(score - top)
            total = jnp.sum(prob, axis=-1, keepdims=True)
            pbuf[lines(h), :] = prob.astype(jnp.bfloat16)
            st2d[lines(h), :] = jnp.where(odd, total, top)

        def weigh(h):
            o2d[lines(h), :] = jnp.dot(
                pbuf[lines(h), :], vbuf[:, lanes(h)], preferred_element_type=jnp.float32
            )

        def message(p, m):
            base, some, lane = starts[p] * rows, sizes[p], lane_of(p)
            stat = None
            for k in range(owned):
                for s in range(2):
                    n = 2 * (m * owned + k) + s
                    x = st2d[pl.ds(base + n, some, stride=rows), :]
                    here = (lane // 16 == k) & (lax.rem(lane, 4) // 2 == s)
                    stat = x if stat is None else jnp.where(here, x, stat)
                    sendb[p][m, 2 * k + s] = o2d[
                        pl.ds(base + n, some, stride=rows), :
                    ].astype(jnp.bfloat16)
            high = stat.astype(jnp.bfloat16).astype(jnp.float32)
            rest = stat - high
            middle = rest.astype(jnp.bfloat16).astype(jnp.float32)
            low = rest - middle
            piece = lax.rem(lane, 16) // 4
            sendb[p][m, 2 * owned] = jnp.where(
                piece == 0, high, jnp.where(piece == 1, middle, low)
            ).astype(jnp.bfloat16)

        for h in range(heads + 2 * LAG):
            if h < heads:
                scores(h)
            if 0 <= h - LAG < heads:
                soften(h - LAG)
            if 0 <= h - 2 * LAG:
                if (h - 2 * LAG) % unit == 0:
                    v_copy((h - 2 * LAG) // unit).wait()
                    w_copy((h - 2 * LAG) // unit).start()
                weigh(h - 2 * LAG)
            if h - 2 * LAG + 1 in starts[1:] + [heads]:
                p = (starts[1:] + [heads]).index(h - 2 * LAG + 1)
                for m in reversed(range(mergers)):
                    message(p, m)

                @pl.when(jnp.logical_not(is_merger))
                def _():
                    for m in reversed(range(mergers)):
                        p_copy(p, m).start()

                @pl.when(is_merger)
                def _():
                    for m in reversed(range(mergers)):

                        @pl.when(me != first + m)
                        def _():
                            p_copy(p, m).start()

                        @pl.when(me == first + m)
                        def _():
                            recvb[p][me] = sendb[p][m]

    group = me - first

    def a_copy(p, to, n):
        return remote(
            xin[p].at[group], xin[p].at[group], a_send.at[p, n], a_recv.at[p, group], "seq", to
        )

    @pl.when(is_merger)
    def combine():
        base = group * owned
        for k in range(owned):

            @pl.when(base + k != me)
            def _():
                for n in range(2):
                    kv_copy(n, k).wait_recv()

        for k in range(owned):
            for n, ref in enumerate((qall.at[base + k], kvown.at[k, 0], kvown.at[k, 1])):
                for h in range(heads):
                    own2d[k, n, 2 * h : 2 * h + 2, :] = ref[:, lanes(h)].astype(jnp.float32)

        def own_terms(k, p):
            some, begin, lane = sizes[p], starts[p], lane_of(p)
            hline = lax.broadcasted_iota(jnp.int32, (some, 1), 0)
            own = [
                [own2d.at[k, n][pl.ds(2 * begin + t, some, stride=2), :] for t in range(2)]
                for n in range(3)
            ]
            slope_col = jnp.zeros((some, 1), jnp.float32)
            for h in range(some):
                slope_col = jnp.where(hline == h, slope_ref[begin + h], slope_col)
            e00 = jnp.sum(own[0][0] * own[1][0], axis=-1, keepdims=True) * scale
            e10 = jnp.sum(own[0][1] * own[1][0], axis=-1, keepdims=True) * scale - slope_col
            e11 = jnp.sum(own[0][1] * own[1][1], axis=-1, keepdims=True) * scale
            upper = jnp.maximum(e10, e11)
            w10 = jnp.exp(e10 - upper)
            w11 = jnp.exp(e11 - upper)
            j = lax.rem(lane, 4)
            stat = jnp.where(
                j == 0, e00, jnp.where(j == 1, 1.0, jnp.where(j == 2, upper, w10 + w11))
            )
            return stat, [own[2][0], w10 * own[2][0] + w11 * own[2][1]]

        own = [[own_terms(k, p) for k in range(owned)] for p in range(parts)]

        def merge(p):
            some, lane = sizes[p], lane_of(p)
            stat = own[p][0][0]
            for k in range(1, owned):
                stat = jnp.where(lane // 16 == k, own[p][k][0], stat)
            stats = [stat]
            for j in range(live):
                x = recvb[p][j, 2 * owned].astype(jnp.float32)
                x = x + pltpu.roll(x, hdim - 4, 1) + pltpu.roll(x, hdim - 8, 1)
                stats.append(x)
            highest = functools.reduce(jnp.maximum, stats)
            factors = [jnp.exp(jnp.minimum(x - highest, 0.0)) for x in stats]
            total = sum(f * pltpu.roll(x, hdim - 1, 1) for f, x in zip(factors, stats))
            inverse = 1.0 / total
            for k in range(owned):
                for s in range(2):
                    c = slice(16 * k + 2 * s, 16 * k + 2 * s + 1)
                    acc = factors[0][:, c] * own[p][k][1][s]
                    for j in range(live):
                        acc += factors[j + 1][:, c] * recvb[p][j, 2 * k + s].astype(jnp.float32)
                    n = k // per * 2 * per + s * per + k % per
                    q2d[pl.ds(n * slot, some), :] = acc * inverse[:, c]
            for h in range(some):
                xin[p][group, :, lanes(h)] = q2d[
                    pl.ds(h, 2 * owned, stride=slot), :
                ].astype(jnp.bfloat16)

        for p in range(parts):
            for step in range(1, live):
                source = to_live(step)
                remote(
                    sendb[p].at[0], recvb[p].at[source], p_send.at[p, 0], p_recv.at[p, source],
                    "seq", source,
                ).wait_recv()
            merge(p)
            for n in range(1, n_seq):
                a_copy(p, other(n - 1), n - 1).start()

    for g in range(groups):
        w_copy(g).wait()

    def h_copy(c, step):
        at = slice(c * tile, (c + 1) * tile)
        return remote(
            shares.at[to_head(step), :, at],
            got.at[step - 1, :, at],
            h_send.at[c, step - 1],
            h_recv.at[c, step - 1],
            "head",
            to_head(step),
        )

    for p in range(parts):
        for m in range(mergers):

            @pl.when(me != first + m)
            def _():
                here = xin[p].at[m]
                remote(
                    here, here, a_send.at[p, 0], a_recv.at[p, m], "seq", first + m
                ).wait_recv()

        x = jnp.concatenate([xin[p][m] for m in range(mergers)], axis=0)
        deep = slice(starts[p] * hdim, (starts[p] + sizes[p]) * hdim)
        for c in range(cols // tile):
            at = slice(c * tile, (c + 1) * tile)
            part = jnp.dot(x, wbuf[deep, at], preferred_element_type=jnp.float32)
            if p > 0:
                part += sofar[:, at]
            if p < parts - 1:
                sofar[:, at] = part
                continue
            for k in range(n_head):
                shares[k, :, at] = part[2 * per * k : 2 * per * (k + 1)].astype(jnp.bfloat16)
            for step in range(1, n_head):
                h_copy(c, step).start()

    @pl.when(is_live)
    def _():
        for step in range(1, live):
            q_copy(step - 1, to_live(step)).wait_send()
        for m in range(mergers):

            @pl.when(me != first + m)
            def _():
                for p in range(parts):
                    p_copy(p, m).wait_send()

    @pl.when(jnp.logical_not(is_live))
    def _():
        for d in range(live):
            q_copy(d, d).wait_send()

    @pl.when(keeper != me)
    def _():
        for n in range(2):
            kv_copy(n, place).wait_send()

    @pl.when(is_merger)
    def _():
        for p in range(parts):
            for n in range(1, n_seq):
                a_copy(p, other(n - 1), n - 1).wait_send()

    summed = shares[mine].astype(jnp.float32)
    for step in range(1, n_head):
        for c in range(cols // tile):
            h_copy(c, step).wait_recv()
        summed += got[step - 1].astype(jnp.float32)
    for s in range(2):
        out_ref[s] = (
            res_ref[s].astype(jnp.float32) + summed[s * per : (s + 1) * per]
        ).astype(jnp.bfloat16)

    for step in range(1, n_head):
        for c in range(cols // tile):
            h_copy(c, step).wait_send()


def body(
    n_seq,
    n_head,
    queries,
    new_keys,
    new_values,
    cache_keys,
    cache_values,
    slopes,
    seg_blocks,
    request_row,
    out_weight,
    residual,
):
    heads = slopes.shape[0]
    width = queries.shape[2]
    hdim = width // heads
    tokens = cache_keys.shape[0]
    cols = out_weight.shape[1]
    assert queries.shape[1] == 1 and seg_blocks.shape[0] == n_seq
    flat = [x.reshape(2, width) for x in (queries, new_keys, new_values)]
    unit = heads // 2
    tile = cols
    rows = 2 * n_seq
    per = n_seq // n_head
    sizes = (heads * 3 // 7, heads * 2 // 7, heads * 2 // 7)
    parts = len(sizes)
    slot = -(-max(sizes) // 8) * 8
    live, first, mergers = 3 * n_seq // 4, 0, n_head
    owned = n_seq // mergers
    assert n_seq % 4 == 0 and owned % per == 0 and 16 * owned <= hdim
    assert sum(sizes) == heads
    groups = heads // unit
    bf16, f32 = jnp.bfloat16, jnp.float32
    dma = pltpu.SemaphoreType.DMA
    vmem = pl.BlockSpec(memory_space=pltpu.VMEM)
    hbm = pl.BlockSpec(memory_space=pl.ANY)
    return pl.pallas_call(
        functools.partial(kernel, n_seq, n_head, heads, unit, tile, live, first, mergers, sizes),
        out_shape=pltpu.VMEM(residual.shape, residual.dtype),
        in_specs=[hbm] * 10,
        out_specs=vmem,
        scratch_shapes=[
            pltpu.VMEM((2, width), bf16),
            pltpu.VMEM((2, width), bf16),
            pltpu.VMEM((2, width), bf16),
            pltpu.SMEM(seg_blocks.shape, jnp.int32),
            pltpu.SMEM(request_row.shape, jnp.int32),
            pltpu.SMEM(slopes.shape, f32),
            pltpu.VMEM(residual.shape, bf16),
            dma((7,)),
            pltpu.VMEM(cache_keys.shape, bf16),
            pltpu.VMEM((width, tokens), bf16),
            pltpu.VMEM(cache_values.shape, bf16),
            pltpu.VMEM(out_weight.shape, bf16),
            pltpu.VMEM((n_seq, 2, width), bf16),
            pltpu.VMEM((owned, 2, 2, width), bf16),
            pltpu.VMEM((owned, 3, 2 * heads, hdim), f32),
            pltpu.VMEM((rows, width), f32),
            pltpu.VMEM((heads * rows, tokens), f32),
            pltpu.VMEM((heads * rows, tokens), bf16),
            pltpu.VMEM((2 * owned * slot, hdim), f32),
            pltpu.VMEM((rows, tokens), f32),
            pltpu.VMEM((heads * rows, hdim), f32),
            pltpu.VMEM((heads * rows, hdim), f32),
            tuple(pltpu.VMEM((mergers, 2 * owned + 1, n, hdim), bf16) for n in sizes),
            tuple(pltpu.VMEM((live, 2 * owned + 1, n, hdim), bf16) for n in sizes),
            tuple(pltpu.VMEM((mergers, 2 * owned, n * hdim), bf16) for n in sizes),
            pltpu.VMEM((rows, cols), f32),
            pltpu.VMEM((n_head, 2 * per, cols), bf16),
            pltpu.VMEM((n_head - 1, 2 * per, cols), bf16),
            dma((groups,)),
            dma((groups,)),
            dma((groups,)),
            dma((live,)),
            dma((n_seq,)),
            dma((2,)),
            dma((owned, 2)),
            dma((parts, mergers)),
            dma((parts, live)),
            dma((parts, n_seq - 1)),
            dma((parts, mergers)),
            dma((cols // tile, n_head - 1)),
            dma((cols // tile, n_head - 1)),
        ],
        compiler_params=pltpu.CompilerParams(
            collective_id=0, has_side_effects=True, vmem_limit_bytes=56 << 20
        ),
    )(*flat, seg_blocks, request_row, slopes, residual, cache_keys, cache_values, out_weight)


def solution(mesh):
    in_specs = (
        P(None, "seq", "head"),
        P(None, "seq", "head"),
        P(None, "seq", "head"),
        P("seq", "head"),
        P("seq", "head"),
        P("head"),
        P(),
        P(),
        P("head", "seq"),
        P(None, "head", "seq"),
    )
    out_specs = P(None, "head", "seq")
    sizes = (mesh.shape["seq"], mesh.shape["head"])
    return jax.shard_map(
        functools.partial(body, *sizes),
        mesh=mesh,
        in_specs=in_specs,
        out_specs=out_specs,
        check_vma=False,
    )
```
